256 devices in a mesh: dp: 32 (over z_lo, x, y), hid: 8 (over z_hi, core).
Axes of the slice: x: 4, y: 4, z: 8 (z_hi: 4, z_lo: 2; z = z_hi * 2 + z_lo), core: 2. Of those that a mesh axis runs over, the one named last changes fastest.
Arguments:
- tokens: bfloat16 [4096, 4096], P('dp', 'hid'), may hold values from -6 to 6
- cotangent: bfloat16 [4096, 4096], P('dp', 'hid'), may hold values from -6 to 6
- routes: int32 [4096, 2], P('dp'), may hold values from 0 to 63, as said below
- gates: float32 [4096, 2], P('dp'), may hold values from 0.2 to 1
- fetch: int32 [32, 2], replicated, may hold values from 0 to 63, as said below
- w_in: bfloat16 [64, 2, 1024, 4096], P('dp', None, 'hid'), may hold values from -0.09375 to 0.09375
- w_down: bfloat16 [64, 1024, 4096], P('dp', 'hid'), may hold values from -0.1875 to 0.1875
Outputs:
- outputs: bfloat16 [4096, 4096], P('dp', 'hid')
- token_grads: bfloat16 [4096, 4096], P('dp', 'hid')
- grad_in: bfloat16 [64, 2, 1024, 4096], P('dp', None, 'hid')
- grad_down: bfloat16 [64, 1024, 4096], P('dp', 'hid')
The draws below stay inside these ranges and needn't reach their ends.
Inputs may be any that keep to these rules, and one draw needn't show every extreme that they name: fetch[r, 0] is an expert owned by dp index r - 1 and fetch[r, 1] one owned by index r + half the dp axis, cyclically; expert e is owned by index e // 2. `routes`: the 2 ids of a token are different candidates of its own dp index (its 2 experts and its two fetched ones); among the tokens of one index no candidate is named more than 96 times, and one is named exactly 96 times.
All inputs are finite; a program needn't handle non-finite values.
Results may differ from the reference program's by a relative error of at most 0.0061.
Values may be sent and summed in bfloat16 or wider, within the bound.
No kernel may reach another device: no remote copies, remote signals or barrier semaphores. Data moves between devices by JAX's collectives and lax.ppermute only.
A program may use at most 128 MiB of HBM per device.

```python
import jax
import jax.numpy as jnp
from jax import lax

D = 4096
FF = 1024
EXP_DEV = 2
TOPK = 2
TOK_DEV = 128
CAP = 96
EXPERTS = 64
TOKENS = 4096
N_DP = 32


def fetch_table(key):
    row_count = EXPERTS // EXP_DEV
    row_ids = jnp.arange(row_count, dtype=jnp.int32)
    picked = jax.random.randint(jax.random.fold_in(key, 11), (row_count, 2), 0, EXP_DEV)
    left_ids = (row_ids - 1) % row_count * EXP_DEV + picked[:, 0]
    far_ids = (row_ids + row_count // 2) % row_count * EXP_DEV + picked[:, 1]
    return jnp.stack([left_ids, far_ids], axis=1).astype(jnp.int32)


def draw_fetch(key, part):
    return fetch_table(key)


def draw_routes(key, part):
    row_count = EXPERTS // EXP_DEV
    table = fetch_table(key)
    base_key = jax.random.fold_in(key, 23)
    cand_count = EXP_DEV + 2

    def one_row(row_index, fetched):
        row_key = jax.random.fold_in(base_key, row_index)
        key_hot, key_rank, key_excl, key_flip = jax.random.split(row_key, 4)
        candidates = jnp.concatenate([row_index * EXP_DEV + jnp.arange(EXP_DEV, dtype=jnp.int32), fetched])
        hot_one = jax.random.randint(key_hot, (), 0, cand_count)
        ranking = jax.random.permutation(key_rank, TOK_DEV)
        others = (hot_one + 1 + jnp.arange(cand_count - 1, dtype=jnp.int32)) % cand_count
        in_hot = ranking < CAP
        second_hot = others[ranking % 3]
        excluded = jax.random.randint(key_excl, (TOK_DEV,), 0, 3)
        first_pick = jnp.where(in_hot, hot_one, others[(excluded + 1) % 3])
        second_pick = jnp.where(in_hot, second_hot, others[(excluded + 2) % 3])
        flipped = jax.random.randint(key_flip, (TOK_DEV,), 0, 2) == 1
        slot_a = jnp.where(flipped, second_pick, first_pick)
        slot_b = jnp.where(flipped, first_pick, second_pick)
        return candidates[jnp.stack([slot_a, slot_b], axis=1)]
    result = jax.vmap(one_row)(jnp.arange(row_count, dtype=jnp.int32), table)
    return result.reshape(row_count * TOK_DEV, TOPK).astype(jnp.int32)


def levels(key, extent, shards, low, largest):
    loudness, own = 1.0, jax.random.fold_in(key, 6)
    for dim, shards_of in shards:
        steps = jnp.exp(jax.random.uniform(jax.random.fold_in(own, dim), (shards_of,), jnp.float32, low / len(shards), largest / len(shards)))
        loudness = loudness * jnp.repeat(steps, extent[dim] // shards_of).reshape([-1 if axis == dim else 1 for axis in range(len(extent))])
    return loudness


def scatter_about(own_key, extent, spread, most, shards=(), kind=jnp.bfloat16):
    values = jax.random.normal(own_key, extent, jnp.float32) * spread
    if len(shards) > 0:
        values = levels(own_key, extent, shards, -0.22, 0.18) * values
    return jnp.clip(values, min=-most, max=most).astype(kind)


def setup_inputs(seed: int = 0) -> dict:
    arg_keys = jax.random.split(jax.random.key(seed), 8)
    return {
        "tokens": scatter_about(arg_keys[0], (TOKENS, D), 1.0, 6.0, ((0, 32), (1, 8))),
        "cotangent": scatter_about(arg_keys[1], (TOKENS, D), 1.0, 6.0, ((0, 32), (1, 8))),
        "routes": draw_routes(jax.random.fold_in(arg_keys[7], 71), 0),
        "gates": jnp.clip(0.2 + 0.8 * jax.random.uniform(arg_keys[3], (TOKENS, TOPK), jnp.float32) ** levels(arg_keys[3], (TOKENS, TOPK), ((0, 32),), -0.2, 0.2), 0.2, 1.0),
        "fetch": draw_fetch(jax.random.fold_in(arg_keys[7], 71), 0),
        "w_in": scatter_about(arg_keys[5], (EXPERTS, 2, FF, D), D ** -0.5, 0.09375, ((0, 32), (2, 8))),
        "w_down": scatter_about(arg_keys[6], (EXPERTS, FF, D), FF ** -0.5, 0.1875, ((0, 32), (1, 8))),
    }


def expert_pass(rows_in, rows_cot, w_pair, w_out):
    contract_last = (((1,), (1,)), ((), ()))
    contract_first = (((0,), (0,)), ((), ()))
    gate_pre = lax.dot_general(rows_in, w_pair[0], contract_last, preferred_element_type=jnp.float32)
    up_proj = lax.dot_general(rows_in, w_pair[1], contract_last, preferred_element_type=jnp.float32)
    sig_gate = 1.0 / (1.0 + jnp.exp(-gate_pre))
    active = gate_pre * sig_gate
    act_slope = sig_gate * (1.0 + gate_pre * (1.0 - sig_gate))
    hidden = (active * up_proj).astype(jnp.bfloat16)
    part_out = jnp.dot(hidden, w_out, preferred_element_type=jnp.float32)
    back_hid = lax.dot_general(rows_cot, w_out, contract_last, preferred_element_type=jnp.float32)
    grad_gate = (back_hid * up_proj * act_slope).astype(jnp.bfloat16)
    grad_up = (back_hid * active).astype(jnp.bfloat16)
    rows_grad = jnp.dot(grad_gate, w_pair[0], preferred_element_type=jnp.float32) + jnp.dot(grad_up, w_pair[1], preferred_element_type=jnp.float32)
    sum_gate = lax.dot_general(grad_gate, rows_in, contract_first, preferred_element_type=jnp.float32)
    sum_up = lax.dot_general(grad_up, rows_in, contract_first, preferred_element_type=jnp.float32)
    sum_down = lax.dot_general(hidden, rows_cot, contract_first, preferred_element_type=jnp.float32)
    return part_out, rows_grad, jnp.stack([sum_gate, sum_up]), sum_down


def reference(tokens, cotangent, routes, gates, fetch, w_in, w_down):
    dp_count = N_DP
    half_way = dp_count // 2

    def row_slice(array, row_index):
        return lax.dynamic_slice_in_dim(array, (row_index * TOK_DEV).astype(jnp.int32), TOK_DEV, 0)

    def weights_for(row_index, expert):
        row_routes = row_slice(routes, row_index)
        row_gates = row_slice(gates, row_index)
        return jnp.sum(jnp.where(row_routes == expert, row_gates, 0.0), axis=1)

    def scaled_rows(row_index, weights):
        row_cot = row_slice(cotangent, row_index)
        return (weights[:, None] * row_cot.astype(jnp.float32)).astype(jnp.bfloat16)

    def row_out(row_index):
        row_x = row_slice(tokens, row_index)
        candidates = jnp.concatenate([row_index * EXP_DEV + jnp.arange(EXP_DEV, dtype=jnp.int32), fetch[row_index].astype(jnp.int32)])
        out_sum = jnp.zeros((TOK_DEV, D), jnp.float32)
        grad_sum = jnp.zeros((TOK_DEV, D), jnp.float32)
        for which in range(EXP_DEV + 2):
            expert = candidates[which]
            weights = weights_for(row_index, expert)
            part_out, rows_grad, unused_in, unused_down = expert_pass(row_x, scaled_rows(row_index, weights), w_in[expert], w_down[expert])
            out_sum = out_sum + weights[:, None] * part_out
            grad_sum = grad_sum + rows_grad
        return out_sum.astype(jnp.bfloat16), grad_sum.astype(jnp.bfloat16)

    outs_rows, grads_rows = lax.map(row_out, jnp.arange(dp_count, dtype=jnp.int32))
    outputs = outs_rows.reshape(TOKENS, D)
    token_grads = grads_rows.reshape(TOKENS, D)

    def expert_grads(expert):
        owner = expert // EXP_DEV
        left_row = (owner + 1) % dp_count
        far_row = (owner + half_way) % dp_count
        sources = ((owner, 1.0), (left_row, (fetch[left_row, 0] == expert).astype(jnp.float32)), (far_row, (fetch[far_row, 1] == expert).astype(jnp.float32)))
        total_in = None
        total_down = None
        for row_index, flag in sources:
            weights = weights_for(row_index, expert) * flag
            row_x = row_slice(tokens, row_index)
            unused_part, unused_rows, term_in, term_down = expert_pass(row_x, scaled_rows(row_index, weights), w_in[expert], w_down[expert])
            if total_in is None:
                total_in = term_in
                total_down = term_down
            else:
                rounded_in, rounded_down = lax.optimization_barrier((term_in.astype(jnp.bfloat16), term_down.astype(jnp.bfloat16)))
                total_in = total_in + rounded_in.astype(jnp.float32)
                total_down = total_down + rounded_down.astype(jnp.float32)
        return total_in.astype(jnp.bfloat16), total_down.astype(jnp.bfloat16)

    grad_in, grad_down = lax.map(expert_grads, jnp.arange(EXPERTS, dtype=jnp.int32))
    return (outputs, token_grads, grad_in, grad_down)
```

```python
import functools

import jax
import jax.numpy as jnp
from jax import lax
from jax.experimental import pallas as pl
from jax.experimental.pallas import tpu as pltpu
from jax.sharding import Mesh
from jax.sharding import PartitionSpec as P

AXES = ("zlo", "x", "y", "zhi", "core")
DP = ("zlo", "x", "y")
HID = ("zhi", "core")
RING = 8
OWN = (4, 2, -2, 0)
FAR = (3, -3, 1, -1)
SLICE = 512
NT = (((1,), (1,)), ((), ()))
TN = (((0,), (0,)), ((), ()))
LIMIT = 56 * 1024 * 1024


def ring_index(z):
    return (z % 2) * 4 + z // 2


def along_z(array, by):
    pairs = [(ring_index(z), ring_index((z + by) % RING)) for z in range(RING)]
    return lax.ppermute(array, ("zlo", "zhi"), pairs)


def along_dp(array, by):
    return lax.ppermute(array, DP, [(i, (i + by) % 32) for i in range(32)])


def other_core(array):
    return lax.ppermute(array, "core", [(0, 1), (1, 0)])


def dot(a, b, dims=None):
    if dims is None:
        return jnp.dot(a, b, preferred_element_type=jnp.float32)
    return lax.dot_general(a, b, dims, preferred_element_type=jnp.float32)


def columns(slot):
    return pl.ds(pl.multiple_of(slot * SLICE, SLICE), SLICE)


def hidden_kernel(where, weights, w_in, w_down, *refs):
    chunks, (hid_ref, hs_ref, grad_ref) = refs[:24], refs[24:]
    own, left, far = chunks[:8], chunks[8:16], chunks[16:]
    need_left, need_far = where[24], where[25]

    def passes(rows, base, expert):
        pre = None
        back = None
        for i, row in enumerate(rows):
            cols = columns(where[base + i])
            p = dot(row[0], w_in[expert, :, cols], NT)
            b = dot(row[1], w_down[expert, :, cols], NT)
            pre = p if pre is None else pre + p
            back = b if back is None else back + b
        return pre, back

    plan = ((own, 0, 0), (own, 0, 1), (left, 8, need_left), (far, 16, need_far))
    for index, (rows, base, expert) in enumerate(plan):
        pre, back = passes(rows, base, expert)
        weight = weights[:, index : index + 1]
        gate_pre, up_proj = pre[:, :128], pre[:, 128:]
        back_hid = weight * back
        sig = 1.0 / (1.0 + jnp.exp(-gate_pre))
        active = gate_pre * sig
        slope = sig * (1.0 + gate_pre * (1.0 - sig))
        hidden = active * up_proj
        hid_ref[index] = hidden.astype(jnp.bfloat16)
        hs_ref[index] = (weight * hidden).astype(jnp.bfloat16)
        grad_ref[index, :, :128] = (back_hid * up_proj * slope).astype(jnp.bfloat16)
        grad_ref[index, :, 128:] = (back_hid * active).astype(jnp.bfloat16)


def rows_kernel(where, weights, w_in, w_down, hid, grad, *outs):
    own, left, far = outs[:8], outs[8:16], outs[16:]
    need_left, need_far = where[24], where[25]
    for i in range(8):
        cols = columns(where[i])
        own[i][0] = (
            weights[:, 0:1] * dot(hid[0], w_down[0, :, cols])
            + weights[:, 1:2] * dot(hid[1], w_down[1, :, cols])
        ).astype(jnp.bfloat16)
        own[i][1] = (
            dot(grad[0], w_in[0, :, cols]) + dot(grad[1], w_in[1, :, cols])
        ).astype(jnp.bfloat16)
        cols = columns(where[8 + i])
        left[i][0] = (weights[:, 2:3] * dot(hid[2], w_down[need_left, :, cols])).astype(jnp.bfloat16)
        left[i][1] = dot(grad[2], w_in[need_left, :, cols]).astype(jnp.bfloat16)
        cols = columns(where[16 + i])
        far[i][0] = (weights[:, 3:4] * dot(hid[3], w_down[need_far, :, cols])).astype(jnp.bfloat16)
        far[i][1] = dot(grad[3], w_in[need_far, :, cols]).astype(jnp.bfloat16)


def weights_kernel(where, hs, grad, *refs):
    chunks, (din_ref, ddown_ref, acc_in, acc_down) = refs[:24], refs[24:]
    need_left, need_far = where[24], where[25]

    def place(base, i):
        return columns(where[base + i])

    def add(expert, cols, index, chunk):
        acc_in[expert, :, cols] += dot(grad[index], chunk[0], TN)
        acc_down[expert, :, cols] += dot(hs[index], chunk[1], TN)

    for i in range(8):
        for expert in range(2):
            acc_in[expert, :, place(0, i)] = dot(grad[expert], chunks[i][0], TN)
            acc_down[expert, :, place(0, i)] = dot(hs[expert], chunks[i][1], TN)
    for i in range(8):
        add(need_left, place(8, i), 2, chunks[8 + i])
    for i in range(8):
        add(need_far, place(16, i), 3, chunks[16 + i])
    for expert in range(2):
        din_ref[expert] = acc_in[expert].astype(jnp.bfloat16)
        ddown_ref[expert] = acc_down[expert].astype(jnp.bfloat16)


SMEM = pl.BlockSpec(memory_space=pltpu.SMEM)
VMEM = pl.BlockSpec(memory_space=pltpu.VMEM)
PARAMS = pltpu.CompilerParams(vmem_limit_bytes=LIMIT)


def shape(*dims, dtype=jnp.bfloat16):
    return jax.ShapeDtypeStruct(dims, dtype)


def shards(tokens, cotangent, routes, gates, fetch, w_in, w_down):
    my_row = lax.axis_index(DP)
    z = lax.axis_index("zhi") * 2 + lax.axis_index("zlo")
    core = lax.axis_index("core")
    both = jnp.stack([tokens, cotangent])

    candidates = jnp.concatenate(
        [my_row * 2 + jnp.arange(2, dtype=jnp.int32), fetch[my_row]]
    )
    matches = routes[:, :, None] == candidates[None, None, :]
    combine = jnp.sum(jnp.where(matches, gates[:, :, None], 0.0), axis=1)
    from_left = along_dp(combine[:, 2:3], -1)
    from_far = along_dp(combine[:, 3:4], 16)
    weights = jnp.concatenate([combine[:, :2], from_left, from_far], axis=1)
    need_left = fetch[(my_row + 1) % 32, 0] - my_row * 2
    need_far = fetch[(my_row + 16) % 32, 1] - my_row * 2

    def slices(offsets):
        same = [((z + k) % RING) // 2 * 2 + core for k in offsets]
        peer = [((z + k) % RING) // 2 * 2 + 1 - core for k in offsets]
        return same + peer

    where = jnp.stack(
        slices(OWN) + slices(OWN) + slices(FAR) + [need_left, need_far]
    ).astype(jnp.int32)

    got = {0: both}
    up = down = both
    for k in (1, 2, 3):
        up, down = along_z(up, 1), along_z(down, -1)
        got[-k], got[k] = up, down
    got[4] = jnp.stack([along_z(up[0], 1), along_z(down[1], -1)])
    own = [got[k] for k in OWN]
    far = [got[k] for k in FAR]
    left = [along_dp(got[k], -1) for k in OWN]
    own = own + [other_core(a) for a in own]
    left = left + [other_core(a) for a in left]
    far = far + [other_core(a) for a in far]
    chunks = own + left + far

    pair = w_in.reshape(2, 256, 4096)
    hid, hs, grad = pl.pallas_call(
        hidden_kernel,
        out_shape=(shape(4, 128, 128), shape(4, 128, 128), shape(4, 128, 256)),
        in_specs=[SMEM] + [VMEM] * 27,
        out_specs=(VMEM, VMEM, VMEM),
        compiler_params=PARAMS,
        name="hidden",
    )(where, weights, pair, w_down, *chunks)
    parts = pl.pallas_call(
        rows_kernel,
        out_shape=tuple(shape(2, 128, SLICE) for _ in range(24)),
        in_specs=[SMEM] + [VMEM] * 5,
        out_specs=tuple(VMEM for _ in range(24)),
        compiler_params=PARAMS,
        name="rows",
    )(where, weights, pair, w_down, hid, grad)
    grad_in, grad_down = pl.pallas_call(
        weights_kernel,
        out_shape=(shape(2, 256, 4096), shape(2, 128, 4096)),
        in_specs=[SMEM] + [VMEM] * 26,
        out_specs=(VMEM, VMEM),
        scratch_shapes=[
            pltpu.VMEM((2, 256, 4096), jnp.float32),
            pltpu.VMEM((2, 128, 4096), jnp.float32),
        ],
        compiler_params=PARAMS,
        name="weights",
    )(where, hs, grad, *chunks)

    def wide(a):
        return a.astype(jnp.float32)

    def narrow(a):
        return a.astype(jnp.bfloat16)

    part = {}
    for i, k in enumerate(OWN):
        lefts = narrow(wide(parts[8 + i]) + wide(other_core(parts[12 + i])))
        part[k] = narrow(
            wide(parts[i]) + wide(other_core(parts[4 + i])) + wide(along_dp(lefts, 1))
        )
    for i, k in enumerate(FAR):
        part[k] = narrow(wide(parts[16 + i]) + wide(other_core(parts[20 + i])))

    up = along_z(part[4][0], 1)
    down = along_z(part[4][1], -1)
    up = jnp.stack([narrow(wide(part[3][0]) + wide(up)), part[3][1]])
    down = jnp.stack([part[-3][0], narrow(wide(part[-3][1]) + wide(down))])
    for k in (2, 1):
        up = narrow(wide(part[k]) + wide(along_z(up, 1)))
        down = narrow(wide(part[-k]) + wide(along_z(down, -1)))
    total = narrow(wide(part[0]) + wide(along_z(up, 1)) + wide(along_z(down, -1)))
    return total[0], total[1], grad_in.reshape(w_in.shape), grad_down


def solution(mesh):
    fine = Mesh(mesh.devices.reshape(2, 4, 4, 4, 2), AXES)
    return jax.shard_map(
        shards,
        mesh=fine,
        in_specs=(
            P(DP, HID),
            P(DP, HID),
            P(DP, None),
            P(DP, None),
            P(),
            P(DP, None, HID, None),
            P(DP, HID, None),
        ),
        out_specs=(
            P(DP, HID),
            P(DP, HID),
            P(DP, None, HID, None),
            P(DP, HID, None),
        ),
        check_vma=False,
    )
```

```python
import jax
import jax.numpy as jnp
from jax import lax
from jax.experimental import pallas as pl
from jax.experimental.pallas import tpu as pltpu
from jax.sharding import Mesh
from jax.sharding import PartitionSpec as P

AXES = ("zlo", "x", "y", "zhi", "core")
DP = ("zlo", "x", "y")
HID = ("zhi", "core")
RING = 8
SLICE = 512
NT = (((1,), (1,)), ((), ()))
MIB = 1024 * 1024
BF = jnp.bfloat16


def ring_index(z):
    return (z % 2) * 4 + z // 2


def along_z(array, by):
    pairs = [(ring_index(z), ring_index((z + by) % RING)) for z in range(RING)]
    return lax.ppermute(array, ("zlo", "zhi"), pairs)


def along_plane(array, by):
    return lax.ppermute(array, ("x", "y"), [(i, (i + by) % 16) for i in range(16)])


def along_dp(array, by):
    return lax.ppermute(array, DP, [(i, (i + by) % 32) for i in range(32)])


def other_core(array):
    return lax.ppermute(array, "core", [(0, 1), (1, 0)])


def together(*arrays):
    return lax.optimization_barrier(arrays)


def wide(a):
    return a.astype(jnp.float32)


def narrow(a):
    return a.astype(BF)


def dot(a, b, dims=None):
    if dims is None:
        return jnp.dot(a, b, preferred_element_type=jnp.float32)
    return lax.dot_general(a, b, dims, preferred_element_type=jnp.float32)


def columns(slot):
    return pl.ds(pl.multiple_of(slot * SLICE, SLICE), SLICE)


def rows_of(expert, height):
    return pl.ds(pl.multiple_of(expert * height, height), height)


def core_of(where, i):
    return where[3] if i < 4 else 1 - where[3]


def near_slot(where, i):
    return ((where[2] + 2 * (i % 4) + 6) % RING) // 2 * 2 + core_of(where, i)


def far_slot(where, i):
    return ((where[2] + 2 * (i % 4) + 5) % RING) // 2 * 2 + core_of(where, i)


def left_slot(where, i):
    return jnp.where(where[4] == 1, far_slot(where, i), near_slot(where, i))


def far_place(where, i):
    quarter = near_slot(where, i) // 2
    low = where[2] % 2
    return ((2 * quarter + 1 - low - where[2] + 3 + RING) % RING) // 2 + i // 4 * 4


def turned(a):
    return narrow(wide(a).T)


def gradients(weight, pre, back, turn, base):
    gate_pre, up_proj = pre[:, :128], pre[:, 128:]
    back_hid = weight * back
    sig = 1.0 / (1.0 + jnp.exp(-gate_pre))
    active = gate_pre * sig
    slope = sig * (1.0 + gate_pre * (1.0 - sig))
    hidden = narrow(weight * (active * up_proj))
    grads = narrow(back_hid * up_proj * slope), narrow(back_hid * active)
    for h, value in enumerate((*grads, hidden)):
        turn[base, 128 * h : 128 * h + 128, :] = turned(value)
    return hidden, grads


def weight_loads(sources, bufs, sems, slot, rows):
    return [
        pltpu.make_async_copy(source.at[row, columns(slot)], buf.at[slot], sem.at[slot])
        for source, buf, sem, row in zip(sources, bufs, sems, rows)
    ]


def chunk_loads(refs, buf, sem):
    return [pltpu.make_async_copy(refs[i], buf.at[i], sem.at[i]) for i in range(8)]


def left_loads(refs, buf, sem):
    copies = []
    for part, base in ((0, 0), (2, 4)):
        for ref, places in zip(refs[part : part + 2], ((1, 2), (0, 3))):
            for h, place in enumerate(places):
                at = base + place
                copies.append(pltpu.make_async_copy(ref.at[h], buf.at[at], sem.at[at]))
    return copies


def projections(buf, slots, w_in, w_down):
    pre = None
    back = None
    for i, slot in enumerate(slots):
        p = dot(buf[i, 0], w_in(slot), NT)
        b = dot(buf[i, 1], w_down(slot), NT)
        pre = p if pre is None else pre + p
        back = b if back is None else back + b
    return pre, back


def row_parts(out, peer, slots, hidden, grads, w_in, w_down):
    for i in (7, 6, 5, 4, 3, 2, 1, 0):
        ref = out if i < 4 else peer
        ref[i % 4, 0] = narrow(dot(hidden, w_down(slots[i])))
        ref[i % 4, 1] = narrow(dot(grads, w_in(slots[i])))


def near_kernel(where, weights, w_in, w_down, *refs):
    own, far = refs[:8], refs[8:16]
    own_out, own_peer, far_out, far_peer, turn = refs[16:21]
    xo, xf, wbuf, dbuf, so, sf, sw, sd = refs[21:]
    own_slots = [near_slot(where, i) for i in range(8)]
    far_slots = [far_slot(where, i) for i in range(8)]
    rows = pl.ds(0, 512), pl.ds(0, 256)
    own_copies = chunk_loads(own, xo, so)
    far_copies = chunk_loads(far, xf, sf)
    matrices = [
        weight_loads((w_in, w_down), (wbuf, dbuf), (sw, sd), slot, rows) for slot in own_slots
    ]
    for copy, pair in zip(own_copies, matrices):
        copy.start()
        for load in pair:
            load.start()
    for copy in far_copies:
        copy.start()
    pre = None
    back = None
    for i, slot in enumerate(own_slots):
        own_copies[i].wait()
        for load in matrices[i]:
            load.wait()
        p = dot(xo[i, 0], wbuf[slot], NT)
        b = dot(xo[i, 1], dbuf[slot], NT)
        pre = p if pre is None else pre + p
        back = b if back is None else back + b
    for copy in far_copies:
        copy.wait()
    first = gradients(weights[:, 0:1], pre[:, :256], back[:, :128], turn, 0)
    second = gradients(weights[:, 1:2], pre[:, 256:], back[:, 128:], turn, 1)
    far_in, far_down = rows_of(where[1], 256), rows_of(where[1], 128)

    def far_w(slot):
        return wbuf[slot, far_in, :]

    def far_d(slot):
        return dbuf[slot, far_down, :]

    pre, back = projections(xf, far_slots, far_w, far_d)
    third = gradients(weights[:, 3:4], pre, back, turn, 2)
    row_parts(
        own_out,
        own_peer,
        own_slots,
        jnp.concatenate([first[0], second[0]], axis=1),
        jnp.concatenate([*first[1], *second[1]], axis=1),
        lambda slot: wbuf[slot],
        lambda slot: dbuf[slot],
    )
    row_parts(
        far_out,
        far_peer,
        far_slots,
        third[0],
        jnp.concatenate(third[1], axis=1),
        far_w,
        far_d,
    )


def left_kernel(where, weights, w_in, w_down, *refs):
    left, (out, peer, turn) = refs[:4], refs[4:7]
    xl, wbuf, dbuf, sl, sw, sd = refs[7:]
    slots = [left_slot(where, i) for i in range(8)]
    rows = rows_of(where[0], 256), rows_of(where[0], 128)
    copies = left_loads(left, xl, sl)
    matrices = [
        weight_loads((w_in, w_down), (wbuf, dbuf), (sw, sd), slot, rows) for slot in slots
    ]
    for copy, pair in zip(copies, matrices):
        copy.start()
        for load in pair:
            load.start()
    for copy in copies:
        copy.wait()
    for pair in matrices:
        for load in pair:
            load.wait()
    pre, back = projections(xl, slots, lambda slot: wbuf[slot], lambda slot: dbuf[slot])
    hidden, grads = gradients(weights[:, 2:3], pre, back, turn, 0)
    row_parts(
        out,
        peer,
        slots,
        hidden,
        jnp.concatenate(grads, axis=1),
        lambda slot: wbuf[slot],
        lambda slot: dbuf[slot],
    )


def weights_kernel(where, turn, left_turn, *refs):
    own, left, far = refs[:8], refs[8:12], refs[12:20]
    din, ddown = refs[20:22]
    xo, xl, xf, sum_in, sum_down, bin_, bdown, so, sl, sf, si, sd = refs[22:]
    copies = chunk_loads(own, xo, so) + left_loads(left, xl, sl) + chunk_loads(far, xf, sf)
    for copy in copies:
        copy.start()
    for copy in copies:
        copy.wait()
    left_in, left_down = rows_of(where[0], 256), rows_of(where[0], 128)
    far_in, far_down = rows_of(where[1], 256), rows_of(where[1], 128)
    started = []
    for i in range(8):
        slot = near_slot(where, i)
        far_at = far_place(where, i)
        left_at = jnp.where(where[4] == 1, far_at, i)
        for e in range(2):
            sum_in[256 * e : 256 * e + 256, :] = dot(turn[e, :256, :], xo[i, 0])
            sum_down[128 * e : 128 * e + 128, :] = dot(turn[e, 256:, :], xo[i, 1])
        sum_in[left_in, :] += dot(left_turn[0, :256, :], xl[left_at, 0])
        sum_down[left_down, :] += dot(left_turn[0, 256:, :], xl[left_at, 1])
        sum_in[far_in, :] += dot(turn[2, :256, :], xf[far_at, 0])
        sum_down[far_down, :] += dot(turn[2, 256:, :], xf[far_at, 1])
        bin_[i] = narrow(sum_in[...])
        bdown[i] = narrow(sum_down[...])
        for copy in (
            pltpu.make_async_copy(bin_.at[i], din.at[:, columns(slot)], si.at[i]),
            pltpu.make_async_copy(bdown.at[i], ddown.at[:, columns(slot)], sd.at[i]),
        ):
            copy.start()
            started.append(copy)
    for copy in started:
        copy.wait()


SMEM = pl.BlockSpec(memory_space=pltpu.SMEM)
VMEM = pl.BlockSpec(memory_space=pltpu.VMEM)
FAR_MEMORY = pl.BlockSpec(memory_space=pltpu.HBM)
DMA = pltpu.SemaphoreType.DMA


def shape(*dims, dtype=BF):
    return jax.ShapeDtypeStruct(dims, dtype)


def params(mib):
    return pltpu.CompilerParams(vmem_limit_bytes=mib * MIB)


QUAD = shape(4, 2, 128, SLICE)
CHUNKS = pltpu.VMEM((8, 2, 128, SLICE), BF)


def shards(tokens, cotangent, routes, gates, fetch, w_in, w_down):
    my_row = lax.axis_index(DP)
    z = lax.axis_index("zhi") * 2 + lax.axis_index("zlo")
    core = lax.axis_index("core")
    plane = my_row % 16
    first, last = plane == 0, plane == 15
    both = jnp.stack([tokens, cotangent])

    candidates = jnp.concatenate(
        [my_row * 2 + jnp.arange(2, dtype=jnp.int32), fetch[my_row]]
    )
    matches = routes[:, :, None] == candidates[None, None, :]
    combine = jnp.sum(jnp.where(matches, gates[:, :, None], 0.0), axis=1)
    need_left = fetch[(my_row + 1) % 32, 0] - my_row * 2
    need_far = fetch[(my_row + 16) % 32, 1] - my_row * 2
    where = jnp.stack([need_left, need_far, z, core, last.astype(jnp.int32)]).astype(jnp.int32)

    def leftward(pairs):
        chosen = [jnp.where(first, got[k - 1], got[k]) for k in pairs]
        return along_plane(jnp.stack(chosen), -1)

    got = {0: both}
    got[-1], got[1] = along_z(both, 1), along_z(both, -1)
    from_far = along_dp(combine[:, 3:4], 16)
    from_left = along_dp(combine[:, 2:3], -1)
    got[-1], got[1], from_far, from_left, where = together(
        got[-1], got[1], from_far, from_left, where
    )
    weights = jnp.concatenate([combine[:, :2], from_left, from_far], axis=1)
    got[-2], got[2] = along_z(got[-1], 1), along_z(got[1], -1)
    got[-2], got[2], weights = together(got[-2], got[2], weights)
    got[-3], got[3] = along_z(got[-2], 1), along_z(got[2], -1)
    early = leftward((0, 2))
    got[-3], got[3] = together(got[-3], got[3])
    up, down = along_z(got[-3][0], 1), along_z(got[3][1], -1)
    up, down, early = together(up, down, early)
    got[4] = jnp.stack([up, down])
    late = leftward((-2, 4))
    own = [got[k] for k in (-2, 0, 2, 4)]
    own = own + [other_core(a) for a in own]
    far = [got[k] for k in (-3, -1, 1, 3)]
    far = far + [other_core(a) for a in far]

    flat_in = w_in.reshape(512, 4096)
    flat_down = w_down.reshape(256, 4096)
    own_out, own_peer, far_out, far_peer, turn = pl.pallas_call(
        near_kernel,
        out_shape=(QUAD,) * 4 + (shape(3, 384, 128),),
        in_specs=[SMEM, VMEM] + [FAR_MEMORY] * 18,
        out_specs=(VMEM,) * 5,
        scratch_shapes=[
            CHUNKS,
            CHUNKS,
            pltpu.VMEM((8, 512, SLICE), BF),
            pltpu.VMEM((8, 256, SLICE), BF),
            DMA((8,)),
            DMA((8,)),
            DMA((8,)),
            DMA((8,)),
        ],
        compiler_params=params(56),
        name="near",
    )(where, weights, flat_in, flat_down, *own, *far)
    late, turn = together(late, turn)
    lefts = [early, late, other_core(early), other_core(late)]
    left_out, left_peer, left_turn = pl.pallas_call(
        left_kernel,
        out_shape=(QUAD,) * 2 + (shape(1, 384, 128),),
        in_specs=[SMEM, VMEM] + [FAR_MEMORY] * 6,
        out_specs=(VMEM,) * 3,
        scratch_shapes=[
            CHUNKS,
            pltpu.VMEM((8, 256, SLICE), BF),
            pltpu.VMEM((8, 128, SLICE), BF),
            DMA((8,)),
            DMA((8,)),
            DMA((8,)),
        ],
        compiler_params=params(56),
        name="left",
    )(where, weights, flat_in, flat_down, *lefts)
    own_peer, far_peer = other_core(own_peer), other_core(far_peer)
    left_peer = other_core(left_peer)

    def rightward(i):
        return along_plane(narrow(wide(left_out[i]) + wide(left_peer[i])), 1)

    right = {3: rightward(3)}
    grad_in, grad_down = pl.pallas_call(
        weights_kernel,
        out_shape=(shape(512, 4096), shape(256, 4096)),
        in_specs=[SMEM, VMEM, VMEM] + [FAR_MEMORY] * 20,
        out_specs=(FAR_MEMORY, FAR_MEMORY),
        scratch_shapes=[
            CHUNKS,
            CHUNKS,
            CHUNKS,
            pltpu.VMEM((512, SLICE), jnp.float32),
            pltpu.VMEM((256, SLICE), jnp.float32),
            pltpu.VMEM((8, 512, SLICE), BF),
            pltpu.VMEM((8, 256, SLICE), BF),
            DMA((8,)),
            DMA((8,)),
            DMA((8,)),
            DMA((8,)),
            DMA((8,)),
        ],
        compiler_params=params(56),
        name="weights",
    )(where, turn, left_turn, *own, *lefts, *far)
    right[3], grad_in, grad_down = together(right[3], grad_in, grad_down)

    def near_part(i, half=slice(None)):
        extra = jnp.where(first, 0.0, wide(right[i][half]))
        return wide(own_out[i][half]) + wide(own_peer[i][half]) + extra

    def far_part(i):
        extra = jnp.where(first, wide(right[i]), 0.0)
        return wide(far_out[i]) + wide(far_peer[i]) + extra

    top = narrow(near_part(3))
    up, down = along_z(top[0], 1), along_z(top[1], -1)
    right[0] = rightward(0)
    up, down, right[0] = together(up, down, right[0])
    high, low = far_part(3), far_part(0)
    up = narrow(jnp.stack([high[0] + wide(up), high[1]]))
    down = narrow(jnp.stack([low[0], low[1] + wide(down)]))
    up, down = along_z(up, 1), along_z(down, -1)
    right[2] = rightward(2)
    up, down, right[2] = together(up, down, right[2])
    up, down = narrow(near_part(2) + wide(up)), narrow(near_part(0) + wide(down))
    up, down = along_z(up, 1), along_z(down, -1)
    right[1] = rightward(1)
    up, down, right[1] = together(up, down, right[1])
    up, down = narrow(far_part(2) + wide(up)), narrow(far_part(1) + wide(down))
    up, down = along_z(up, 1), along_z(down, -1)
    total = narrow(near_part(1) + wide(up) + wide(down))
    return total[0], total[1], grad_in.reshape(w_in.shape), grad_down.reshape(w_down.shape)


def solution(mesh):
    fine = Mesh(mesh.devices.reshape(2, 4, 4, 4, 2), AXES)
    return jax.shard_map(
        shards,
        mesh=fine,
        in_specs=(
            P(DP, HID),
            P(DP, HID),
            P(DP, None),
            P(DP, None),
            P(),
            P(DP, None, HID, None),
            P(DP, HID, None),
        ),
        out_specs=(
            P(DP, HID),
            P(DP, HID),
            P(DP, None, HID, None),
            P(DP, HID, None),
        ),
        check_vma=False,
    )
```

```python
import jax
import jax.numpy as jnp
from jax import lax
from jax.experimental import pallas as pl
from jax.experimental.pallas import tpu as pltpu
from jax.sharding import Mesh
from jax.sharding import PartitionSpec as P

AXES = ("zlo", "x", "y", "zhi", "core")
DP = ("zlo", "x", "y")
HID = ("zhi", "core")
RING = 8
SLICE = 512
NT = (((1,), (1,)), ((), ()))
MIB = 1024 * 1024
BF = jnp.bfloat16


def ring_index(z):
    return (z % 2) * 4 + z // 2


def along_z(array, by):
    pairs = [(ring_index(z), ring_index((z + by) % RING)) for z in range(RING)]
    return lax.ppermute(array, ("zlo", "zhi"), pairs)


def along_plane(array, by):
    return lax.ppermute(array, ("x", "y"), [(i, (i + by) % 16) for i in range(16)])


def along_dp(array, by):
    return lax.ppermute(array, DP, [(i, (i + by) % 32) for i in range(32)])


def other_core(array):
    return lax.ppermute(array, "core", [(0, 1), (1, 0)])


def together(*arrays):
    return lax.optimization_barrier(arrays)


def wide(a):
    return a.astype(jnp.float32)


def narrow(a):
    return a.astype(BF)


def dot(a, b, dims=None):
    if dims is None:
        return jnp.dot(a, b, preferred_element_type=jnp.float32)
    return lax.dot_general(a, b, dims, preferred_element_type=jnp.float32)


def columns(slot):
    return pl.ds(pl.multiple_of(slot * SLICE, SLICE), SLICE)


def rows_of(expert, height):
    return pl.ds(pl.multiple_of(expert * height, height), height)


def core_of(where, i):
    return where[3] if i < 4 else 1 - where[3]


def near_slot(where, i):
    return ((where[2] + 2 * (i % 4) + 6) % RING) // 2 * 2 + core_of(where, i)


def far_slot(where, i):
    return ((where[2] + 2 * (i % 4) + 5) % RING) // 2 * 2 + core_of(where, i)


def left_slot(where, i):
    return jnp.where(where[4] == 1, far_slot(where, i), near_slot(where, i))


def far_place(where, i):
    quarter = near_slot(where, i) // 2
    low = where[2] % 2
    return ((2 * quarter + 1 - low - where[2] + 3 + RING) % RING) // 2 + i // 4 * 4


def turned(a):
    return narrow(wide(a).T)


def gradients(weight, pre, back, turn, base):
    gate_pre, up_proj = pre[:, :128], pre[:, 128:]
    back_hid = weight * back
    sig = 1.0 / (1.0 + jnp.exp(-gate_pre))
    active = gate_pre * sig
    slope = sig * (1.0 + gate_pre * (1.0 - sig))
    hidden = narrow(weight * (active * up_proj))
    grads = narrow(back_hid * up_proj * slope), narrow(back_hid * active)
    for h, value in enumerate((*grads, hidden)):
        turn[base, 128 * h : 128 * h + 128, :] = turned(value)
    return hidden, grads


def weight_loads(sources, bufs, sems, slot, rows):
    return [
        pltpu.make_async_copy(source.at[row, columns(slot)], buf.at[slot], sem.at[slot])
        for source, buf, sem, row in zip(sources, bufs, sems, rows)
    ]


def chunk_loads(refs, buf, sem):
    return [pltpu.make_async_copy(refs[i], buf.at[i], sem.at[i]) for i in range(8)]


def left_loads(refs, buf, sem):
    copies = []
    for part, base in ((0, 0), (2, 4)):
        for ref, places in zip(refs[part : part + 2], ((1, 2), (0, 3))):
            for h, place in enumerate(places):
                at = base + place
                copies.append(pltpu.make_async_copy(ref.at[h], buf.at[at], sem.at[at]))
    return copies


def projections(buf, slots, w_in, w_down):
    pre = None
    back = None
    for i, slot in enumerate(slots):
        p = dot(buf[i, 0], w_in(slot), NT)
        b = dot(buf[i, 1], w_down(slot), NT)
        pre = p if pre is None else pre + p
        back = b if back is None else back + b
    return pre, back


def row_parts(out, peer, slots, hidden, grads, w_in, w_down):
    for i in (7, 6, 5, 4, 3, 2, 1, 0):
        ref = out if i < 4 else peer
        ref[i % 4, 0] = narrow(dot(hidden, w_down(slots[i])))
        ref[i % 4, 1] = narrow(dot(grads, w_in(slots[i])))


def near_kernel(where, weights, w_in, w_down, *refs):
    own, far = refs[:8], refs[8:16]
    own_out, own_peer, far_out, far_peer, turn = refs[16:21]
    xo, xf, wbuf, dbuf, so, sf, sw, sd = refs[21:]
    own_slots = [near_slot(where, i) for i in range(8)]
    far_slots = [far_slot(where, i) for i in range(8)]
    rows = pl.ds(0, 512), pl.ds(0, 256)
    own_copies = chunk_loads(own, xo, so)
    far_copies = chunk_loads(far, xf, sf)
    matrices = [
        weight_loads((w_in, w_down), (wbuf, dbuf), (sw, sd), slot, rows) for slot in own_slots
    ]
    for copy, pair in zip(own_copies, matrices):
        copy.start()
        for load in pair:
            load.start()
    for copy in far_copies:
        copy.start()
    pre = None
    back = None
    for i, slot in enumerate(own_slots):
        own_copies[i].wait()
        for load in matrices[i]:
            load.wait()
        p = dot(xo[i, 0], wbuf[slot], NT)
        b = dot(xo[i, 1], dbuf[slot], NT)
        pre = p if pre is None else pre + p
        back = b if back is None else back + b
    for copy in far_copies:
        copy.wait()
    first = gradients(weights[:, 0:1], pre[:, :256], back[:, :128], turn, 0)
    second = gradients(weights[:, 1:2], pre[:, 256:], back[:, 128:], turn, 1)
    far_in, far_down = rows_of(where[1], 256), rows_of(where[1], 128)

    def far_w(slot):
        return wbuf[slot, far_in, :]

    def far_d(slot):
        return dbuf[slot, far_down, :]

    pre, back = projections(xf, far_slots, far_w, far_d)
    third = gradients(weights[:, 3:4], pre, back, turn, 2)
    row_parts(
        own_out,
        own_peer,
        own_slots,
        jnp.concatenate([first[0], second[0]], axis=1),
        jnp.concatenate([*first[1], *second[1]], axis=1),
        lambda slot: wbuf[slot],
        lambda slot: dbuf[slot],
    )
    row_parts(
        far_out,
        far_peer,
        far_slots,
        third[0],
        jnp.concatenate(third[1], axis=1),
        far_w,
        far_d,
    )


def left_kernel(where, weights, w_in, w_down, *refs):
    left, (out, peer, turn) = refs[:4], refs[4:7]
    xl, wbuf, dbuf, sl, sw, sd = refs[7:]
    slots = [left_slot(where, i) for i in range(8)]
    rows = rows_of(where[0], 256), rows_of(where[0], 128)
    copies = left_loads(left, xl, sl)
    matrices = [
        weight_loads((w_in, w_down), (wbuf, dbuf), (sw, sd), slot, rows) for slot in slots
    ]
    for copy, pair in zip(copies, matrices):
        copy.start()
        for load in pair:
            load.start()
    for copy in copies:
        copy.wait()
    pre = None
    back = None
    for i, slot in enumerate(slots):
        for load in matrices[i]:
            load.wait()
        p = dot(xl[i, 0], wbuf[slot], NT)
        b = dot(xl[i, 1], dbuf[slot], NT)
        pre = p if pre is None else pre + p
        back = b if back is None else back + b
    hidden, grads = gradients(weights[:, 2:3], pre, back, turn, 0)
    row_parts(
        out,
        peer,
        slots,
        hidden,
        jnp.concatenate(grads, axis=1),
        lambda slot: wbuf[slot],
        lambda slot: dbuf[slot],
    )


def weights_kernel(where, turn, left_turn, *refs):
    own, left, far = refs[:8], refs[8:12], refs[12:20]
    din, ddown = refs[20:22]
    xo, xl, xf, sum_in, sum_down, bin_, bdown, so, sl, sf, si, sd = refs[22:]
    copies = chunk_loads(own, xo, so) + left_loads(left, xl, sl) + chunk_loads(far, xf, sf)
    for copy in copies:
        copy.start()
    for copy in copies:
        copy.wait()
    left_in, left_down = rows_of(where[0], 256), rows_of(where[0], 128)
    far_in, far_down = rows_of(where[1], 256), rows_of(where[1], 128)
    started = []
    for i in range(8):
        slot = near_slot(where, i)
        far_at = far_place(where, i)
        left_at = jnp.where(where[4] == 1, far_at, i)
        for e in range(2):
            sum_in[256 * e : 256 * e + 256, :] = dot(turn[e, :256, :], xo[i, 0])
            sum_down[128 * e : 128 * e + 128, :] = dot(turn[e, 256:, :], xo[i, 1])
        sum_in[left_in, :] += dot(left_turn[0, :256, :], xl[left_at, 0])
        sum_down[left_down, :] += dot(left_turn[0, 256:, :], xl[left_at, 1])
        sum_in[far_in, :] += dot(turn[2, :256, :], xf[far_at, 0])
        sum_down[far_down, :] += dot(turn[2, 256:, :], xf[far_at, 1])
        bin_[i] = narrow(sum_in[...])
        bdown[i] = narrow(sum_down[...])
        for copy in (
            pltpu.make_async_copy(bin_.at[i], din.at[:, columns(slot)], si.at[i]),
            pltpu.make_async_copy(bdown.at[i], ddown.at[:, columns(slot)], sd.at[i]),
        ):
            copy.start()
            started.append(copy)
    for copy in started:
        copy.wait()


SMEM = pl.BlockSpec(memory_space=pltpu.SMEM)
VMEM = pl.BlockSpec(memory_space=pltpu.VMEM)
FAR_MEMORY = pl.BlockSpec(memory_space=pltpu.HBM)
DMA = pltpu.SemaphoreType.DMA


def shape(*dims, dtype=BF):
    return jax.ShapeDtypeStruct(dims, dtype)


def in_hbm(a):
    return pltpu.with_memory_space_constraint(a, pltpu.HBM)


def params(mib):
    return pltpu.CompilerParams(vmem_limit_bytes=mib * MIB)


QUAD = shape(4, 2, 128, SLICE)
CHUNKS = pltpu.VMEM((8, 2, 128, SLICE), BF)


def shards(tokens, cotangent, routes, gates, fetch, w_in, w_down):
    my_row = lax.axis_index(DP)
    z = lax.axis_index("zhi") * 2 + lax.axis_index("zlo")
    core = lax.axis_index("core")
    plane = my_row % 16
    first, last = plane == 0, plane == 15
    both = jnp.stack([tokens, cotangent])

    candidates = jnp.concatenate(
        [my_row * 2 + jnp.arange(2, dtype=jnp.int32), fetch[my_row]]
    )
    matches = routes[:, :, None] == candidates[None, None, :]
    combine = jnp.sum(jnp.where(matches, gates[:, :, None], 0.0), axis=1)
    need_left = fetch[(my_row + 1) % 32, 0] - my_row * 2
    need_far = fetch[(my_row + 16) % 32, 1] - my_row * 2
    where = jnp.stack([need_left, need_far, z, core, last.astype(jnp.int32)]).astype(jnp.int32)

    def leftward(pairs):
        chosen = [jnp.where(first, got[k - 1], got[k]) for k in pairs]
        return along_plane(jnp.stack(chosen), -1)

    got = {0: both}
    got[-1], got[1] = along_z(both, 1), along_z(both, -1)
    from_far = along_dp(combine[:, 2:4], 16)
    got[-1], got[1], from_far, where = together(got[-1], got[1], from_far, where)
    got[-2], got[2] = along_z(got[-1], 1), along_z(got[1], -1)
    from_left = along_plane(jnp.where(first, from_far[:, 0:1], combine[:, 2:3]), -1)
    got[-2], got[2], from_left = together(got[-2], got[2], from_left)
    weights = jnp.concatenate([combine[:, :2], from_left, from_far[:, 1:2]], axis=1)
    got[-3], got[3] = along_z(got[-2], 1), along_z(got[2], -1)
    early = leftward((0, 2))
    got[-3], got[3], weights = together(got[-3], got[3], weights)
    up, down = along_z(got[-3][0], 1), along_z(got[3][1], -1)
    up, down, early = together(up, down, early)
    got[4] = jnp.stack([up, down])
    late = leftward((-2, 4))
    own = [got[k] for k in (-2, 0, 2, 4)]
    own = own + [other_core(a) for a in own]
    far = [got[k] for k in (-3, -1, 1, 3)]
    far = far + [other_core(a) for a in far]

    flat_in = in_hbm(w_in.reshape(512, 4096))
    flat_down = in_hbm(w_down.reshape(256, 4096))
    own_out, own_peer, far_out, far_peer, turn = pl.pallas_call(
        near_kernel,
        out_shape=(QUAD,) * 4 + (shape(3, 384, 128),),
        in_specs=[SMEM, VMEM] + [FAR_MEMORY] * 18,
        out_specs=(VMEM,) * 5,
        scratch_shapes=[
            CHUNKS,
            CHUNKS,
            pltpu.VMEM((8, 512, SLICE), BF),
            pltpu.VMEM((8, 256, SLICE), BF),
            DMA((8,)),
            DMA((8,)),
            DMA((8,)),
            DMA((8,)),
        ],
        compiler_params=params(20),
        name="near",
    )(where, weights, flat_in, flat_down, *own, *far)
    late, turn = together(late, turn)
    lefts = [early, late, other_core(early), other_core(late)]
    left_out, left_peer, left_turn = pl.pallas_call(
        left_kernel,
        out_shape=(QUAD,) * 2 + (shape(1, 384, 128),),
        in_specs=[SMEM, VMEM] + [FAR_MEMORY] * 6,
        out_specs=(VMEM,) * 3,
        scratch_shapes=[
            CHUNKS,
            pltpu.VMEM((8, 256, SLICE), BF),
            pltpu.VMEM((8, 128, SLICE), BF),
            DMA((8,)),
            DMA((8,)),
            DMA((8,)),
        ],
        compiler_params=params(12),
        name="left",
    )(where, weights, flat_in, flat_down, *lefts)
    own_peer, far_peer = other_core(own_peer), other_core(far_peer)
    left_peer = other_core(left_peer)

    def rightward(i):
        return along_plane(narrow(wide(left_out[i]) + wide(left_peer[i])), 1)

    right = {3: rightward(3)}
    grad_in, grad_down = pl.pallas_call(
        weights_kernel,
        out_shape=(shape(512, 4096), shape(256, 4096)),
        in_specs=[SMEM, VMEM, VMEM] + [FAR_MEMORY] * 20,
        out_specs=(FAR_MEMORY, FAR_MEMORY),
        scratch_shapes=[
            CHUNKS,
            CHUNKS,
            CHUNKS,
            pltpu.VMEM((512, SLICE), jnp.float32),
            pltpu.VMEM((256, SLICE), jnp.float32),
            pltpu.VMEM((8, 512, SLICE), BF),
            pltpu.VMEM((8, 256, SLICE), BF),
            DMA((8,)),
            DMA((8,)),
            DMA((8,)),
            DMA((8,)),
            DMA((8,)),
        ],
        compiler_params=params(20),
        name="weights",
    )(where, turn, left_turn, *own, *lefts, *far)
    right[3], grad_in, grad_down = together(right[3], grad_in, grad_down)

    def near_part(i, half=slice(None)):
        extra = jnp.where(first, 0.0, wide(right[i][half]))
        return wide(own_out[i][half]) + wide(own_peer[i][half]) + extra

    def far_part(i):
        extra = jnp.where(first, wide(right[i]), 0.0)
        return wide(far_out[i]) + wide(far_peer[i]) + extra

    top = narrow(near_part(3))
    up, down = along_z(top[0], 1), along_z(top[1], -1)
    right[0] = rightward(0)
    up, down, right[0] = together(up, down, right[0])
    high, low = far_part(3), far_part(0)
    up = narrow(jnp.stack([high[0] + wide(up), high[1]]))
    down = narrow(jnp.stack([low[0], low[1] + wide(down)]))
    up, down = along_z(up, 1), along_z(down, -1)
    right[2] = rightward(2)
    up, down, right[2] = together(up, down, right[2])
    up, down = narrow(near_part(2) + wide(up)), narrow(near_part(0) + wide(down))
    up, down = along_z(up, 1), along_z(down, -1)
    right[1] = rightward(1)
    up, down, right[1] = together(up, down, right[1])
    up, down = narrow(far_part(2) + wide(up)), narrow(far_part(1) + wide(down))
    up, down = along_z(up, 1), along_z(down, -1)
    total = narrow(near_part(1) + wide(up) + wide(down))
    return total[0], total[1], grad_in.reshape(w_in.shape), grad_down.reshape(w_down.shape)


def solution(mesh):
    fine = Mesh(mesh.devices.reshape(2, 4, 4, 4, 2), AXES)
    return jax.shard_map(
        shards,
        mesh=fine,
        in_specs=(
            P(DP, HID),
            P(DP, HID),
            P(DP, None),
            P(DP, None),
            P(),
            P(DP, None, HID, None),
            P(DP, HID, None),
        ),
        out_specs=(
            P(DP, HID),
            P(DP, HID),
            P(DP, None, HID, None),
            P(DP, HID, None),
        ),
        check_vma=False,
    )
```

```python
import jax
import jax.numpy as jnp
from jax import lax
from jax.experimental import pallas as pl
from jax.experimental.pallas import tpu as pltpu
from jax.sharding import Mesh
from jax.sharding import PartitionSpec as P

AXES = ("zlo", "x", "y", "zhi", "core")
DP = ("zlo", "x", "y")
HID = ("zhi", "core")
RING = 8
SLICE = 512
NT = (((1,), (1,)), ((), ()))
MIB = 1024 * 1024
BF = jnp.bfloat16


def ring_index(z):
    return (z % 2) * 4 + z // 2


def along_z(array, by):
    pairs = [(ring_index(z), ring_index((z + by) % RING)) for z in range(RING)]
    return lax.ppermute(array, ("zlo", "zhi"), pairs)


def along_plane(array, by):
    return lax.ppermute(array, ("x", "y"), [(i, (i + by) % 16) for i in range(16)])


def along_dp(array, by):
    return lax.ppermute(array, DP, [(i, (i + by) % 32) for i in range(32)])


def other_core(array):
    return lax.ppermute(array, "core", [(0, 1), (1, 0)])


def together(*arrays):
    return lax.optimization_barrier(arrays)


def wide(a):
    return a.astype(jnp.float32)


def narrow(a):
    return a.astype(BF)


def dot(a, b, dims=None):
    if dims is None:
        return jnp.dot(a, b, preferred_element_type=jnp.float32)
    return lax.dot_general(a, b, dims, preferred_element_type=jnp.float32)


def columns(slot):
    return pl.ds(pl.multiple_of(slot * SLICE, SLICE), SLICE)


def rows_of(expert, height):
    return pl.ds(pl.multiple_of(expert * height, height), height)


def core_of(where, i):
    return jnp.where(i < 4, where[3], 1 - where[3])


def near_slot(where, i):
    return ((where[2] + 2 * (i % 4) + 6) % RING) // 2 * 2 + core_of(where, i)


def far_slot(where, i):
    return ((where[2] + 2 * (i % 4) + 5) % RING) // 2 * 2 + core_of(where, i)


def left_slot(where, i):
    return jnp.where(where[4] == 1, far_slot(where, i), near_slot(where, i))


def far_place(where, i):
    quarter = near_slot(where, i) // 2
    low = where[2] % 2
    return ((2 * quarter + 1 - low - where[2] + 3 + RING) % RING) // 2 + i // 4 * 4


def turned(a):
    return narrow(wide(a).T)


def gradients(weight, pre, back, turn, base):
    gate_pre, up_proj = pre[:, :128], pre[:, 128:]
    back_hid = weight * back
    sig = 1.0 / (1.0 + jnp.exp(-gate_pre))
    active = gate_pre * sig
    slope = sig * (1.0 + gate_pre * (1.0 - sig))
    hidden = narrow(weight * (active * up_proj))
    grads = narrow(back_hid * up_proj * slope), narrow(back_hid * active)
    for h, value in enumerate((*grads, hidden)):
        turn[base, 128 * h : 128 * h + 128, :] = turned(value)
    return hidden, grads


def weight_loads(sources, bufs, sems, slot, rows):
    return [
        pltpu.make_async_copy(source.at[row, columns(slot)], buf.at[slot], sem.at[slot])
        for source, buf, sem, row in zip(sources, bufs, sems, rows)
    ]


def chunk_loads(refs, buf, sem):
    return [pltpu.make_async_copy(refs[i], buf.at[i], sem.at[i]) for i in range(8)]


def left_loads(refs, buf, sem):
    copies = []
    for part, base in ((0, 0), (2, 4)):
        for ref, places in zip(refs[part : part + 2], ((1, 2), (0, 3))):
            for h, place in enumerate(places):
                at = base + place
                copies.append(pltpu.make_async_copy(ref.at[h], buf.at[at], sem.at[at]))
    return copies


def projections(buf, slots, w_in, w_down):
    pre = None
    back = None
    for i, slot in enumerate(slots):
        p = dot(buf[i, 0], w_in(slot), NT)
        b = dot(buf[i, 1], w_down(slot), NT)
        pre = p if pre is None else pre + p
        back = b if back is None else back + b
    return pre, back


def row_parts(out, peer, slots, hidden, grads, w_in, w_down):
    for i in (7, 6, 5, 4, 3, 2, 1, 0):
        ref = out if i < 4 else peer
        ref[i % 4, 0] = narrow(dot(hidden, w_down(slots[i])))
        ref[i % 4, 1] = narrow(dot(grads, w_in(slots[i])))


def near_kernel(where, weights, w_in, w_down, *refs):
    own, far = refs[:8], refs[8:16]
    own_out, own_peer, far_out, far_peer, turn = refs[16:21]
    xo, xf, wbuf, dbuf, so, sf, sw, sd = refs[21:]
    own_slots = [near_slot(where, i) for i in range(8)]
    far_slots = [far_slot(where, i) for i in range(8)]
    rows = pl.ds(0, 512), pl.ds(0, 256)
    own_copies = chunk_loads(own, xo, so)
    far_copies = chunk_loads(far, xf, sf)
    matrices = [
        weight_loads((w_in, w_down), (wbuf, dbuf), (sw, sd), slot, rows) for slot in own_slots
    ]
    for copy, pair in zip(own_copies, matrices):
        copy.start()
        for load in pair:
            load.start()
    for copy in far_copies:
        copy.start()
    pre = None
    back = None
    for i, slot in enumerate(own_slots):
        own_copies[i].wait()
        for load in matrices[i]:
            load.wait()
        p = dot(xo[i, 0], wbuf[slot], NT)
        b = dot(xo[i, 1], dbuf[slot], NT)
        pre = p if pre is None else pre + p
        back = b if back is None else back + b
    for copy in far_copies:
        copy.wait()
    first = gradients(weights[:, 0:1], pre[:, :256], back[:, :128], turn, 0)
    second = gradients(weights[:, 1:2], pre[:, 256:], back[:, 128:], turn, 1)
    far_in, far_down = rows_of(where[1], 256), rows_of(where[1], 128)

    def far_w(slot):
        return wbuf[slot, far_in, :]

    def far_d(slot):
        return dbuf[slot, far_down, :]

    pre, back = projections(xf, far_slots, far_w, far_d)
    third = gradients(weights[:, 3:4], pre, back, turn, 2)
    row_parts(
        own_out,
        own_peer,
        own_slots,
        jnp.concatenate([first[0], second[0]], axis=1),
        jnp.concatenate([*first[1], *second[1]], axis=1),
        lambda slot: wbuf[slot],
        lambda slot: dbuf[slot],
    )
    row_parts(
        far_out,
        far_peer,
        far_slots,
        third[0],
        jnp.concatenate(third[1], axis=1),
        far_w,
        far_d,
    )


def left_kernel(where, weights, w_in, w_down, *refs):
    left, (out, peer, turn) = refs[:4], refs[4:7]
    xl, wbuf, dbuf, sl, sw, sd = refs[7:]
    slots = [left_slot(where, i) for i in range(8)]
    rows = rows_of(where[0], 256), rows_of(where[0], 128)
    copies = left_loads(left, xl, sl)
    matrices = [
        weight_loads((w_in, w_down), (wbuf, dbuf), (sw, sd), slot, rows) for slot in slots
    ]
    for copy, pair in zip(copies, matrices):
        copy.start()
        for load in pair:
            load.start()
    for copy in copies:
        copy.wait()
    pre = None
    back = None
    for i, slot in enumerate(slots):
        for load in matrices[i]:
            load.wait()
        p = dot(xl[i, 0], wbuf[slot], NT)
        b = dot(xl[i, 1], dbuf[slot], NT)
        pre = p if pre is None else pre + p
        back = b if back is None else back + b
    hidden, grads = gradients(weights[:, 2:3], pre, back, turn, 0)
    row_parts(
        out,
        peer,
        slots,
        hidden,
        jnp.concatenate(grads, axis=1),
        lambda slot: wbuf[slot],
        lambda slot: dbuf[slot],
    )


def weights_kernel(where, turn, left_turn, *refs):
    own, left, far = refs[:8], refs[8:12], refs[12:20]
    din, ddown = refs[20:22]
    xo, xl, xf, sum_in, sum_down, bin_, bdown, so, sl, sf, si, sd = refs[22:]
    copies = chunk_loads(own, xo, so) + left_loads(left, xl, sl) + chunk_loads(far, xf, sf)
    for copy in copies:
        copy.start()
    for copy in copies:
        copy.wait()
    left_in, left_down = rows_of(where[0], 256), rows_of(where[0], 128)
    far_in, far_down = rows_of(where[1], 256), rows_of(where[1], 128)

    def stores(i):
        cols = columns(near_slot(where, i))
        return (
            pltpu.make_async_copy(bin_.at[i], din.at[:, cols], si.at[i]),
            pltpu.make_async_copy(bdown.at[i], ddown.at[:, cols], sd.at[i]),
        )

    def step(i, carry):
        far_at = far_place(where, i)
        left_at = jnp.where(where[4] == 1, far_at, i)
        for e in range(2):
            sum_in[256 * e : 256 * e + 256, :] = dot(turn[e, :256, :], xo[i, 0])
            sum_down[128 * e : 128 * e + 128, :] = dot(turn[e, 256:, :], xo[i, 1])
        sum_in[left_in, :] += dot(left_turn[0, :256, :], xl[left_at, 0])
        sum_down[left_down, :] += dot(left_turn[0, 256:, :], xl[left_at, 1])
        sum_in[far_in, :] += dot(turn[2, :256, :], xf[far_at, 0])
        sum_down[far_down, :] += dot(turn[2, 256:, :], xf[far_at, 1])
        bin_[i] = narrow(sum_in[...])
        bdown[i] = narrow(sum_down[...])
        for copy in stores(i):
            copy.start()
        return carry

    def finish(i, carry):
        for copy in stores(i):
            copy.wait()
        return carry

    lax.fori_loop(0, 8, step, 0)
    lax.fori_loop(0, 8, finish, 0)


SMEM = pl.BlockSpec(memory_space=pltpu.SMEM)
VMEM = pl.BlockSpec(memory_space=pltpu.VMEM)
FAR_MEMORY = pl.BlockSpec(memory_space=pltpu.HBM)
DMA = pltpu.SemaphoreType.DMA


def shape(*dims, dtype=BF):
    return jax.ShapeDtypeStruct(dims, dtype)


def in_hbm(a):
    return pltpu.with_memory_space_constraint(a, pltpu.HBM)


def params(mib):
    return pltpu.CompilerParams(vmem_limit_bytes=mib * MIB)


QUAD = shape(4, 2, 128, SLICE)
CHUNKS = pltpu.VMEM((8, 2, 128, SLICE), BF)


def shards(tokens, cotangent, routes, gates, fetch, w_in, w_down):
    my_row = lax.axis_index(DP)
    z = lax.axis_index("zhi") * 2 + lax.axis_index("zlo")
    core = lax.axis_index("core")
    plane = my_row % 16
    first, last = plane == 0, plane == 15
    both = jnp.stack([tokens, cotangent])

    candidates = jnp.concatenate(
        [my_row * 2 + jnp.arange(2, dtype=jnp.int32), fetch[my_row]]
    )
    matches = routes[:, :, None] == candidates[None, None, :]
    combine = jnp.sum(jnp.where(matches, gates[:, :, None], 0.0), axis=1)
    need_left = fetch[(my_row + 1) % 32, 0] - my_row * 2
    need_far = fetch[(my_row + 16) % 32, 1] - my_row * 2
    where = jnp.stack([need_left, need_far, z, core, last.astype(jnp.int32)]).astype(jnp.int32)

    def leftward(pairs):
        chosen = [jnp.where(first, got[k - 1], got[k]) for k in pairs]
        return along_plane(jnp.stack(chosen), -1)

    got = {0: both}
    got[-1], got[1] = along_z(both, 1), along_z(both, -1)
    from_far = along_dp(combine[:, 2:4], 16)
    got[-1], got[1], from_far, where = together(got[-1], got[1], from_far, where)
    got[-2], got[2] = along_z(got[-1], 1), along_z(got[1], -1)
    from_left = along_plane(jnp.where(first, from_far[:, 0:1], combine[:, 2:3]), -1)
    got[-2], got[2], from_left = together(got[-2], got[2], from_left)
    weights = jnp.concatenate([combine[:, :2], from_left, from_far[:, 1:2]], axis=1)
    got[-3], got[3] = along_z(got[-2], 1), along_z(got[2], -1)
    early = leftward((0, 2))
    got[-3], got[3], weights = together(got[-3], got[3], weights)
    up, down = along_z(got[-3][0], 1), along_z(got[3][1], -1)
    up, down, early = together(up, down, early)
    got[4] = jnp.stack([up, down])
    own = [got[k] for k in (-2, 0, 2, 4)]
    far = [got[k] for k in (-3, -1, 1, 3)]
    own_peers = [other_core(a) for a in own]
    far_peers = [other_core(a) for a in far]
    got[4], *own_peers = together(got[4], *own_peers)
    own = own[:3] + [got[4]] + [in_hbm(a) for a in own_peers]
    far = far + [in_hbm(a) for a in far_peers]
    late = leftward((-2, 4))

    flat_in = in_hbm(w_in.reshape(512, 4096))
    flat_down = in_hbm(w_down.reshape(256, 4096))
    own_out, own_peer, far_out, far_peer, turn = pl.pallas_call(
        near_kernel,
        out_shape=(QUAD,) * 4 + (shape(3, 384, 128),),
        in_specs=[SMEM, VMEM] + [FAR_MEMORY] * 18,
        out_specs=(VMEM,) * 5,
        scratch_shapes=[
            CHUNKS,
            CHUNKS,
            pltpu.VMEM((8, 512, SLICE), BF),
            pltpu.VMEM((8, 256, SLICE), BF),
            DMA((8,)),
            DMA((8,)),
            DMA((8,)),
            DMA((8,)),
        ],
        compiler_params=params(16),
        name="near",
    )(where, weights, flat_in, flat_down, *own, *far)
    late, turn = together(late, turn)
    lefts = [early, late, other_core(early), other_core(late)]
    left_out, left_peer, left_turn = pl.pallas_call(
        left_kernel,
        out_shape=(QUAD,) * 2 + (shape(1, 384, 128),),
        in_specs=[SMEM, VMEM] + [FAR_MEMORY] * 6,
        out_specs=(VMEM,) * 3,
        scratch_shapes=[
            CHUNKS,
            pltpu.VMEM((8, 256, SLICE), BF),
            pltpu.VMEM((8, 128, SLICE), BF),
            DMA((8,)),
            DMA((8,)),
            DMA((8,)),
        ],
        compiler_params=params(10),
        name="left",
    )(where, weights, flat_in, flat_down, *lefts)
    own_peer, far_peer = other_core(own_peer), other_core(far_peer)
    left_peer = other_core(left_peer)

    def rightward(i):
        return along_plane(narrow(wide(left_out[i]) + wide(left_peer[i])), 1)

    right = {3: rightward(3)}
    grad_in, grad_down = pl.pallas_call(
        weights_kernel,
        out_shape=(shape(512, 4096), shape(256, 4096)),
        in_specs=[SMEM, VMEM, VMEM] + [FAR_MEMORY] * 20,
        out_specs=(FAR_MEMORY, FAR_MEMORY),
        scratch_shapes=[
            CHUNKS,
            CHUNKS,
            CHUNKS,
            pltpu.VMEM((512, SLICE), jnp.float32),
            pltpu.VMEM((256, SLICE), jnp.float32),
            pltpu.VMEM((8, 512, SLICE), BF),
            pltpu.VMEM((8, 256, SLICE), BF),
            DMA((8,)),
            DMA((8,)),
            DMA((8,)),
            DMA((8,)),
            DMA((8,)),
        ],
        compiler_params=params(16),
        name="weights",
    )(where, turn, left_turn, *own, *lefts, *far)
    right[3], grad_in, grad_down = together(right[3], grad_in, grad_down)

    def near_part(i, half=slice(None)):
        extra = jnp.where(first, 0.0, wide(right[i][half]))
        return wide(own_out[i][half]) + wide(own_peer[i][half]) + extra

    def far_part(i):
        extra = jnp.where(first, wide(right[i]), 0.0)
        return wide(far_out[i]) + wide(far_peer[i]) + extra

    top = narrow(near_part(3))
    up, down = along_z(top[0], 1), along_z(top[1], -1)
    right[0] = rightward(0)
    up, down, right[0] = together(up, down, right[0])
    high, low = far_part(3), far_part(0)
    up = narrow(jnp.stack([high[0] + wide(up), high[1]]))
    down = narrow(jnp.stack([low[0], low[1] + wide(down)]))
    up, down = along_z(up, 1), along_z(down, -1)
    right[2] = rightward(2)
    up, down, right[2] = together(up, down, right[2])
    up, down = narrow(near_part(2) + wide(up)), narrow(near_part(0) + wide(down))
    up, down = along_z(up, 1), along_z(down, -1)
    right[1] = rightward(1)
    up, down, right[1] = together(up, down, right[1])
    up, down = narrow(far_part(2) + wide(up)), narrow(far_part(1) + wide(down))
    up, down = along_z(up, 1), along_z(down, -1)
    total = narrow(near_part(1) + wide(up) + wide(down))
    return total[0], total[1], grad_in.reshape(w_in.shape), grad_down.reshape(w_down.shape)


def solution(mesh):
    fine = Mesh(mesh.devices.reshape(2, 4, 4, 4, 2), AXES)
    return jax.shard_map(
        shards,
        mesh=fine,
        in_specs=(
            P(DP, HID),
            P(DP, HID),
            P(DP, None),
            P(DP, None),
            P(),
            P(DP, None, HID, None),
            P(DP, HID, None),
        ),
        out_specs=(
            P(DP, HID),
            P(DP, HID),
            P(DP, None, HID, None),
            P(DP, HID, None),
        ),
        check_vma=False,
    )
```

```python
import jax
import jax.numpy as jnp
from jax import lax
from jax.experimental import pallas as pl
from jax.experimental.pallas import tpu as pltpu
from jax.sharding import Mesh
from jax.sharding import PartitionSpec as P

AXES = ("zlo", "x", "y", "zhi", "core")
DP = ("zlo", "x", "y")
HID = ("zhi", "core")
RING = 8
SLICE = 512
NT = (((1,), (1,)), ((), ()))
MIB = 1024 * 1024
BF = jnp.bfloat16


def ring_index(z):
    return (z % 2) * 4 + z // 2


def along_z(array, by):
    pairs = [(ring_index(z), ring_index((z + by) % RING)) for z in range(RING)]
    return lax.ppermute(array, ("zlo", "zhi"), pairs)


def along_plane(array, by):
    return lax.ppermute(array, ("x", "y"), [(i, (i + by) % 16) for i in range(16)])


def along_dp(array, by):
    return lax.ppermute(array, DP, [(i, (i + by) % 32) for i in range(32)])


def other_core(array):
    return lax.ppermute(array, "core", [(0, 1), (1, 0)])


def together(*arrays):
    return lax.optimization_barrier(arrays)


def wide(a):
    return a.astype(jnp.float32)


def narrow(a):
    return a.astype(BF)


def dot(a, b, dims=None):
    if dims is None:
        return jnp.dot(a, b, preferred_element_type=jnp.float32)
    return lax.dot_general(a, b, dims, preferred_element_type=jnp.float32)


def columns(slot):
    return pl.ds(pl.multiple_of(slot * SLICE, SLICE), SLICE)


def rows_of(expert, height):
    return pl.ds(pl.multiple_of(expert * height, height), height)


def core_of(where, i):
    return jnp.where(i < 4, where[3], 1 - where[3])


def near_slot(where, i):
    return ((where[2] + 2 * (i % 4) + 6) % RING) // 2 * 2 + core_of(where, i)


def far_slot(where, i):
    return ((where[2] + 2 * (i % 4) + 5) % RING) // 2 * 2 + core_of(where, i)


def left_slot(where, i):
    return jnp.where(where[4] == 1, far_slot(where, i), near_slot(where, i))


def far_place(where, i):
    quarter = near_slot(where, i) // 2
    low = where[2] % 2
    return ((2 * quarter + 1 - low - where[2] + 3 + RING) % RING) // 2 + i // 4 * 4


def turned(a):
    return narrow(wide(a).T)


def gradients(weight, pre, back, turn, base):
    gate_pre, up_proj = pre[:, :128], pre[:, 128:]
    back_hid = weight * back
    sig = 1.0 / (1.0 + jnp.exp(-gate_pre))
    active = gate_pre * sig
    slope = sig * (1.0 + gate_pre * (1.0 - sig))
    hidden = narrow(weight * (active * up_proj))
    grads = narrow(back_hid * up_proj * slope), narrow(back_hid * active)
    for h, value in enumerate((*grads, hidden)):
        turn[base, 128 * h : 128 * h + 128, :] = turned(value)
    return hidden, grads


def weight_loads(sources, bufs, sems, slot, rows):
    return [
        pltpu.make_async_copy(source.at[row, columns(slot)], buf.at[slot], sem.at[slot])
        for source, buf, sem, row in zip(sources, bufs, sems, rows)
    ]


def chunk_loads(refs, buf, sem):
    return [pltpu.make_async_copy(refs[i], buf.at[i], sem.at[i]) for i in range(8)]


def left_loads(refs, buf, sem):
    copies = []
    for part, base in ((0, 0), (2, 4)):
        for ref, places in zip(refs[part : part + 2], ((1, 2), (0, 3))):
            for h, place in enumerate(places):
                at = base + place
                copies.append(pltpu.make_async_copy(ref.at[h], buf.at[at], sem.at[at]))
    return copies


def projections(buf, slots, w_in, w_down):
    pre = None
    back = None
    for i, slot in enumerate(slots):
        p = dot(buf[i, 0], w_in(slot), NT)
        b = dot(buf[i, 1], w_down(slot), NT)
        pre = p if pre is None else pre + p
        back = b if back is None else back + b
    return pre, back


def row_parts(out, peer, slots, hidden, grads, w_in, w_down):
    for i in (7, 6, 5, 4, 3, 2, 1, 0):
        ref = out if i < 4 else peer
        ref[i % 4, 0] = narrow(dot(hidden, w_down(slots[i])))
        ref[i % 4, 1] = narrow(dot(grads, w_in(slots[i])))


def near_kernel(where, weights, w_in, w_down, *refs):
    own, far = refs[:8], refs[8:16]
    own_out, own_peer, far_out, far_peer, turn = refs[16:21]
    xo, xf, wbuf, dbuf, so, sf, sw, sd = refs[21:]
    own_slots = [near_slot(where, i) for i in range(8)]
    far_slots = [far_slot(where, i) for i in range(8)]
    rows = pl.ds(0, 512), pl.ds(0, 256)
    own_copies = chunk_loads(own, xo, so)
    far_copies = chunk_loads(far, xf, sf)
    matrices = [
        weight_loads((w_in, w_down), (wbuf, dbuf), (sw, sd), slot, rows) for slot in own_slots
    ]
    for copy, pair in zip(own_copies, matrices):
        copy.start()
        for load in pair:
            load.start()
    for copy in far_copies:
        copy.start()
    pre = None
    back = None
    for i, slot in enumerate(own_slots):
        own_copies[i].wait()
        for load in matrices[i]:
            load.wait()
        p = dot(xo[i, 0], wbuf[slot], NT)
        b = dot(xo[i, 1], dbuf[slot], NT)
        pre = p if pre is None else pre + p
        back = b if back is None else back + b
    for copy in far_copies:
        copy.wait()
    first = gradients(weights[:, 0:1], pre[:, :256], back[:, :128], turn, 0)
    second = gradients(weights[:, 1:2], pre[:, 256:], back[:, 128:], turn, 1)
    far_in, far_down = rows_of(where[1], 256), rows_of(where[1], 128)

    def far_w(slot):
        return wbuf[slot, far_in, :]

    def far_d(slot):
        return dbuf[slot, far_down, :]

    pre, back = projections(xf, far_slots, far_w, far_d)
    third = gradients(weights[:, 3:4], pre, back, turn, 2)
    row_parts(
        own_out,
        own_peer,
        own_slots,
        jnp.concatenate([first[0], second[0]], axis=1),
        jnp.concatenate([*first[1], *second[1]], axis=1),
        lambda slot: wbuf[slot],
        lambda slot: dbuf[slot],
    )
    row_parts(
        far_out,
        far_peer,
        far_slots,
        third[0],
        jnp.concatenate(third[1], axis=1),
        far_w,
        far_d,
    )


def left_kernel(where, weights, w_in, w_down, *refs):
    left, (out, peer, turn) = refs[:4], refs[4:7]
    xl, wbuf, dbuf, sl, sw, sd = refs[7:]
    slots = [left_slot(where, i) for i in range(8)]
    rows = rows_of(where[0], 256), rows_of(where[0], 128)
    copies = left_loads(left, xl, sl)
    matrices = [
        weight_loads((w_in, w_down), (wbuf, dbuf), (sw, sd), slot, rows) for slot in slots
    ]
    for copy, pair in zip(copies, matrices):
        copy.start()
        for load in pair:
            load.start()
    for copy in copies:
        copy.wait()
    pre = None
    back = None
    for i, slot in enumerate(slots):
        for load in matrices[i]:
            load.wait()
        p = dot(xl[i, 0], wbuf[slot], NT)
        b = dot(xl[i, 1], dbuf[slot], NT)
        pre = p if pre is None else pre + p
        back = b if back is None else back + b
    hidden, grads = gradients(weights[:, 2:3], pre, back, turn, 0)
    row_parts(
        out,
        peer,
        slots,
        hidden,
        jnp.concatenate(grads, axis=1),
        lambda slot: wbuf[slot],
        lambda slot: dbuf[slot],
    )


def weights_kernel(where, turn, left_turn, *refs):
    own, left, far = refs[:8], refs[8:12], refs[12:20]
    din, ddown = refs[20:22]
    xo, xl, xf, sum_in, sum_down, bin_, bdown, so, sl, sf, si, sd = refs[22:]
    copies = chunk_loads(own, xo, so) + left_loads(left, xl, sl) + chunk_loads(far, xf, sf)
    for copy in copies:
        copy.start()
    for copy in copies:
        copy.wait()
    left_in, left_down = rows_of(where[0], 256), rows_of(where[0], 128)
    far_in, far_down = rows_of(where[1], 256), rows_of(where[1], 128)

    def stores(i):
        cols = columns(near_slot(where, i))
        return (
            pltpu.make_async_copy(bin_.at[i], din.at[:, cols], si.at[i]),
            pltpu.make_async_copy(bdown.at[i], ddown.at[:, cols], sd.at[i]),
        )

    def step(i, carry):
        far_at = far_place(where, i)
        left_at = jnp.where(where[4] == 1, far_at, i)
        for e in range(2):
            sum_in[256 * e : 256 * e + 256, :] = dot(turn[e, :256, :], xo[i, 0])
            sum_down[128 * e : 128 * e + 128, :] = dot(turn[e, 256:, :], xo[i, 1])
        sum_in[left_in, :] += dot(left_turn[0, :256, :], xl[left_at, 0])
        sum_down[left_down, :] += dot(left_turn[0, 256:, :], xl[left_at, 1])
        sum_in[far_in, :] += dot(turn[2, :256, :], xf[far_at, 0])
        sum_down[far_down, :] += dot(turn[2, 256:, :], xf[far_at, 1])
        bin_[i] = narrow(sum_in[...])
        bdown[i] = narrow(sum_down[...])
        for copy in stores(i):
            copy.start()
        return carry

    def finish(i, carry):
        for copy in stores(i):
            copy.wait()
        return carry

    lax.fori_loop(0, 8, step, 0)
    lax.fori_loop(0, 8, finish, 0)


SMEM = pl.BlockSpec(memory_space=pltpu.SMEM)
VMEM = pl.BlockSpec(memory_space=pltpu.VMEM)
FAR_MEMORY = pl.BlockSpec(memory_space=pltpu.HBM)
DMA = pltpu.SemaphoreType.DMA


def shape(*dims, dtype=BF):
    return jax.ShapeDtypeStruct(dims, dtype)


def in_hbm(a):
    return pltpu.with_memory_space_constraint(a, pltpu.HBM)


def params(mib):
    return pltpu.CompilerParams(vmem_limit_bytes=mib * MIB)


QUAD = shape(4, 2, 128, SLICE)
CHUNKS = pltpu.VMEM((8, 2, 128, SLICE), BF)


def shards(tokens, cotangent, routes, gates, fetch, w_in, w_down):
    my_row = lax.axis_index(DP)
    z = lax.axis_index("zhi") * 2 + lax.axis_index("zlo")
    core = lax.axis_index("core")
    plane = my_row % 16
    first, last = plane == 0, plane == 15
    both = jnp.stack([tokens, cotangent])

    candidates = jnp.concatenate(
        [my_row * 2 + jnp.arange(2, dtype=jnp.int32), fetch[my_row]]
    )
    matches = routes[:, :, None] == candidates[None, None, :]
    combine = jnp.sum(jnp.where(matches, gates[:, :, None], 0.0), axis=1)
    need_left = fetch[(my_row + 1) % 32, 0] - my_row * 2
    need_far = fetch[(my_row + 16) % 32, 1] - my_row * 2
    where = jnp.stack([need_left, need_far, z, core, last.astype(jnp.int32)]).astype(jnp.int32)

    def leftward(pairs):
        chosen = [jnp.where(first, got[k - 1], got[k]) for k in pairs]
        return along_plane(jnp.stack(chosen), -1)

    got = {0: both}
    got[-1], got[1] = along_z(both, 1), along_z(both, -1)
    from_far = along_dp(combine[:, 2:4], 16)
    got[-1], got[1], from_far, where = together(got[-1], got[1], from_far, where)
    got[-2], got[2] = along_z(got[-1], 1), along_z(got[1], -1)
    from_left = along_plane(jnp.where(first, from_far[:, 0:1], combine[:, 2:3]), -1)
    got[-2], got[2], from_left = together(got[-2], got[2], from_left)
    weights = jnp.concatenate([combine[:, :2], from_left, from_far[:, 1:2]], axis=1)
    got[-3], got[3] = along_z(got[-2], 1), along_z(got[2], -1)
    early = leftward((0, 2))
    got[-3], got[3], weights = together(got[-3], got[3], weights)
    up, down = along_z(got[-3][0], 1), along_z(got[3][1], -1)
    up, down, early = together(up, down, early)
    got[4] = jnp.stack([up, down])
    own = [got[k] for k in (-2, 0, 2, 4)]
    far = [got[k] for k in (-3, -1, 1, 3)]
    own_peers = [other_core(a) for a in own]
    far_peers = [other_core(a) for a in far]
    got[4], *own_peers = together(got[4], *own_peers)
    own = own[:3] + [got[4]] + [in_hbm(a) for a in own_peers]
    far = far + [in_hbm(a) for a in far_peers]
    late = leftward((-2, 4))

    flat_in = in_hbm(w_in.reshape(512, 4096))
    flat_down = in_hbm(w_down.reshape(256, 4096))
    own_out, own_peer, far_out, far_peer, turn = pl.pallas_call(
        near_kernel,
        out_shape=(QUAD,) * 4 + (shape(3, 384, 128),),
        in_specs=[SMEM, VMEM] + [FAR_MEMORY] * 18,
        out_specs=(VMEM,) * 5,
        scratch_shapes=[
            CHUNKS,
            CHUNKS,
            pltpu.VMEM((8, 512, SLICE), BF),
            pltpu.VMEM((8, 256, SLICE), BF),
            DMA((8,)),
            DMA((8,)),
            DMA((8,)),
            DMA((8,)),
        ],
        compiler_params=params(16),
        name="near",
    )(where, weights, flat_in, flat_down, *own, *far)
    late, turn = together(late, turn)
    lefts = [early, late, other_core(early), other_core(late)]
    left_out, left_peer, left_turn = pl.pallas_call(
        left_kernel,
        out_shape=(QUAD,) * 2 + (shape(1, 384, 128),),
        in_specs=[SMEM, VMEM] + [FAR_MEMORY] * 6,
        out_specs=(VMEM,) * 3,
        scratch_shapes=[
            CHUNKS,
            pltpu.VMEM((8, 256, SLICE), BF),
            pltpu.VMEM((8, 128, SLICE), BF),
            DMA((8,)),
            DMA((8,)),
            DMA((8,)),
        ],
        compiler_params=params(10),
        name="left",
    )(where, weights, flat_in, flat_down, *lefts)
    own_peer, far_peer = other_core(own_peer), other_core(far_peer)
    left_peer = other_core(left_peer)

    def left_sum(i):
        return wide(left_out[i]) + wide(left_peer[i])

    def rightward(sums):
        return along_plane(narrow(sums), 1)

    right = {0: rightward(left_sum(0))}
    moved = lax.ppermute(narrow(left_sum(3)), "zhi", [(i, (i + 2) % 4) for i in range(4)])
    grad_in, grad_down = pl.pallas_call(
        weights_kernel,
        out_shape=(shape(512, 4096), shape(256, 4096)),
        in_specs=[SMEM, VMEM, VMEM] + [FAR_MEMORY] * 20,
        out_specs=(FAR_MEMORY, FAR_MEMORY),
        scratch_shapes=[
            CHUNKS,
            CHUNKS,
            CHUNKS,
            pltpu.VMEM((512, SLICE), jnp.float32),
            pltpu.VMEM((256, SLICE), jnp.float32),
            pltpu.VMEM((8, 512, SLICE), BF),
            pltpu.VMEM((8, 256, SLICE), BF),
            DMA((8,)),
            DMA((8,)),
            DMA((8,)),
            DMA((8,)),
            DMA((8,)),
        ],
        compiler_params=params(16),
        name="weights",
    )(where, turn, left_turn, *own, *lefts, *far)

    def near_part(i):
        part = wide(own_out[i]) + wide(own_peer[i])
        return part + jnp.where(first, 0.0, wide(right[i])) if i in right else part

    def far_part(i):
        part = wide(far_out[i]) + wide(far_peer[i])
        return part + jnp.where(first, wide(right[i]), 0.0) if i in right else part

    top = narrow(near_part(3))
    up, down = along_z(top[0], 1), along_z(top[1], -1)
    up, down, right[0], grad_in, grad_down = together(up, down, right[0], grad_in, grad_down)
    high, low = far_part(3), far_part(0)
    up = narrow(jnp.stack([high[0] + wide(up), high[1]]))
    down = narrow(jnp.stack([low[0], low[1] + wide(down)]))
    up, down = along_z(up, 1), along_z(down, -1)
    right[2] = rightward(left_sum(2))
    up, down, right[2], moved = together(up, down, right[2], moved)
    up, down = narrow(near_part(2) + wide(up)), narrow(near_part(0) + wide(down))
    up, down = along_z(up, 1), along_z(down, -1)
    right[1] = rightward(left_sum(1) + wide(moved))
    up, down, right[1] = together(up, down, right[1])
    up, down = narrow(far_part(2) + wide(up)), narrow(far_part(1) + wide(down))
    up, down = along_z(up, 1), along_z(down, -1)
    total = narrow(near_part(1) + wide(up) + wide(down))
    return total[0], total[1], grad_in.reshape(w_in.shape), grad_down.reshape(w_down.shape)


def solution(mesh):
    fine = Mesh(mesh.devices.reshape(2, 4, 4, 4, 2), AXES)
    return jax.shard_map(
        shards,
        mesh=fine,
        in_specs=(
            P(DP, HID),
            P(DP, HID),
            P(DP, None),
            P(DP, None),
            P(),
            P(DP, None, HID, None),
            P(DP, HID, None),
        ),
        out_specs=(
            P(DP, HID),
            P(DP, HID),
            P(DP, None, HID, None),
            P(DP, HID, None),
        ),
        check_vma=False,
    )
```

```python
import jax
import jax.numpy as jnp
from jax import lax
from jax.experimental import pallas as pl
from jax.experimental.pallas import tpu as pltpu
from jax.sharding import Mesh
from jax.sharding import PartitionSpec as P

AXES = ("zlo", "x", "y", "zhi", "core")
DP = ("zlo", "x", "y")
HID = ("zhi", "core")
RING = 8
SLICE = 512
NT = (((1,), (1,)), ((), ()))
MIB = 1024 * 1024
BF = jnp.bfloat16


def ring_index(z):
    return (z % 2) * 4 + z // 2


def along_z(array, by):
    pairs = [(ring_index(z), ring_index((z + by) % RING)) for z in range(RING)]
    return lax.ppermute(array, ("zlo", "zhi"), pairs)


def along_plane(array, by):
    return lax.ppermute(array, ("x", "y"), [(i, (i + by) % 16) for i in range(16)])


def along_dp(array, by):
    return lax.ppermute(array, DP, [(i, (i + by) % 32) for i in range(32)])


def other_core(array):
    return lax.ppermute(array, "core", [(0, 1), (1, 0)])


def together(*arrays):
    return lax.optimization_barrier(arrays)


def wide(a):
    return a.astype(jnp.float32)


def narrow(a):
    return a.astype(BF)


def dot(a, b, dims=None):
    if dims is None:
        return jnp.dot(a, b, preferred_element_type=jnp.float32)
    return lax.dot_general(a, b, dims, preferred_element_type=jnp.float32)


def columns(slot):
    return pl.ds(pl.multiple_of(slot * SLICE, SLICE), SLICE)


def rows_of(expert, height):
    return pl.ds(pl.multiple_of(expert * height, height), height)


def core_of(where, i):
    return jnp.where(i < 4, where[3], 1 - where[3])


def near_slot(where, i):
    return ((where[2] + 2 * (i % 4) + 6) % RING) // 2 * 2 + core_of(where, i)


def far_slot(where, i):
    return ((where[2] + 2 * (i % 4) + 5) % RING) // 2 * 2 + core_of(where, i)


def left_slot(where, i):
    return jnp.where(where[4] == 1, far_slot(where, i), near_slot(where, i))


def far_place(where, i):
    quarter = near_slot(where, i) // 2
    low = where[2] % 2
    return ((2 * quarter + 1 - low - where[2] + 3 + RING) % RING) // 2 + i // 4 * 4


def turned(a):
    return narrow(wide(a).T)


def gradients(weight, pre, back, turn, base):
    gate_pre, up_proj = pre[:, :128], pre[:, 128:]
    back_hid = weight * back
    sig = 1.0 / (1.0 + jnp.exp(-gate_pre))
    active = gate_pre * sig
    slope = sig * (1.0 + gate_pre * (1.0 - sig))
    hidden = narrow(weight * (active * up_proj))
    grads = narrow(back_hid * up_proj * slope), narrow(back_hid * active)
    for h, value in enumerate((*grads, hidden)):
        turn[base, 128 * h : 128 * h + 128, :] = turned(value)
    return hidden, grads


def weight_loads(sources, bufs, sems, slot, rows):
    return [
        pltpu.make_async_copy(source.at[row, columns(slot)], buf.at[slot], sem.at[slot])
        for source, buf, sem, row in zip(sources, bufs, sems, rows)
    ]


def chunk_loads(refs, buf, sem):
    return [pltpu.make_async_copy(refs[i], buf.at[i], sem.at[i]) for i in range(8)]


def left_loads(refs, buf, sem):
    copies = []
    for part, base in ((0, 0), (2, 4)):
        for ref, places in zip(refs[part : part + 2], ((1, 2), (0, 3))):
            for h, place in enumerate(places):
                at = base + place
                copies.append(pltpu.make_async_copy(ref.at[h], buf.at[at], sem.at[at]))
    return copies


def projections(buf, slots, w_in, w_down):
    pre = None
    back = None
    for i, slot in enumerate(slots):
        p = dot(buf[i, 0], w_in(slot), NT)
        b = dot(buf[i, 1], w_down(slot), NT)
        pre = p if pre is None else pre + p
        back = b if back is None else back + b
    return pre, back


def row_parts(out, peer, slots, hidden, grads, w_in, w_down):
    for i in (7, 6, 5, 4, 3, 2, 1, 0):
        ref = out if i < 4 else peer
        ref[i % 4, 0] = narrow(dot(hidden, w_down(slots[i])))
        ref[i % 4, 1] = narrow(dot(grads, w_in(slots[i])))


def near_kernel(where, weights, w_in, w_down, *refs):
    own, far = refs[:8], refs[8:16]
    own_out, own_peer, far_out, far_peer, turn = refs[16:21]
    xo, xf, wbuf, dbuf, so, sf, sw, sd = refs[21:]
    own_slots = [near_slot(where, i) for i in range(8)]
    far_slots = [far_slot(where, i) for i in range(8)]
    rows = pl.ds(0, 512), pl.ds(0, 256)
    own_copies = chunk_loads(own, xo, so)
    far_copies = chunk_loads(far, xf, sf)
    matrices = [
        weight_loads((w_in, w_down), (wbuf, dbuf), (sw, sd), slot, rows) for slot in own_slots
    ]
    for copy, pair in zip(own_copies, matrices):
        copy.start()
        for load in pair:
            load.start()
    for copy in far_copies:
        copy.start()
    pre = None
    back = None
    for i, slot in enumerate(own_slots):
        own_copies[i].wait()
        for load in matrices[i]:
            load.wait()
        p = dot(xo[i, 0], wbuf[slot], NT)
        b = dot(xo[i, 1], dbuf[slot], NT)
        pre = p if pre is None else pre + p
        back = b if back is None else back + b
    for copy in far_copies:
        copy.wait()
    first = gradients(weights[:, 0:1], pre[:, :256], back[:, :128], turn, 0)
    second = gradients(weights[:, 1:2], pre[:, 256:], back[:, 128:], turn, 1)
    far_in, far_down = rows_of(where[1], 256), rows_of(where[1], 128)

    def far_w(slot):
        return wbuf[slot, far_in, :]

    def far_d(slot):
        return dbuf[slot, far_down, :]

    pre, back = projections(xf, far_slots, far_w, far_d)
    third = gradients(weights[:, 3:4], pre, back, turn, 2)
    row_parts(
        own_out,
        own_peer,
        own_slots,
        jnp.concatenate([first[0], second[0]], axis=1),
        jnp.concatenate([*first[1], *second[1]], axis=1),
        lambda slot: wbuf[slot],
        lambda slot: dbuf[slot],
    )
    row_parts(
        far_out,
        far_peer,
        far_slots,
        third[0],
        jnp.concatenate(third[1], axis=1),
        far_w,
        far_d,
    )


def left_kernel(where, weights, w_in, w_down, *refs):
    left, (out, peer, turn) = refs[:4], refs[4:7]
    xl, wbuf, dbuf, sl, sw, sd = refs[7:]
    slots = [left_slot(where, i) for i in range(8)]
    rows = rows_of(where[0], 256), rows_of(where[0], 128)
    copies = left_loads(left, xl, sl)
    matrices = [
        weight_loads((w_in, w_down), (wbuf, dbuf), (sw, sd), slot, rows) for slot in slots
    ]
    for copy, pair in zip(copies, matrices):
        copy.start()
        for load in pair:
            load.start()
    for copy in copies:
        copy.wait()
    pre = None
    back = None
    for i, slot in enumerate(slots):
        for load in matrices[i]:
            load.wait()
        p = dot(xl[i, 0], wbuf[slot], NT)
        b = dot(xl[i, 1], dbuf[slot], NT)
        pre = p if pre is None else pre + p
        back = b if back is None else back + b
    hidden, grads = gradients(weights[:, 2:3], pre, back, turn, 0)
    row_parts(
        out,
        peer,
        slots,
        hidden,
        jnp.concatenate(grads, axis=1),
        lambda slot: wbuf[slot],
        lambda slot: dbuf[slot],
    )


def weights_kernel(where, turn, left_turn, *refs):
    own, left, far = refs[:8], refs[8:12], refs[12:20]
    din, ddown = refs[20:22]
    xo, xl, xf, sum_in, sum_down, bin_, bdown, so, sl, sf, si, sd = refs[22:]
    copies = chunk_loads(own, xo, so) + left_loads(left, xl, sl) + chunk_loads(far, xf, sf)
    for copy in copies:
        copy.start()
    for copy in copies:
        copy.wait()
    left_in, left_down = rows_of(where[0], 256), rows_of(where[0], 128)
    far_in, far_down = rows_of(where[1], 256), rows_of(where[1], 128)

    def stores(i):
        cols = columns(near_slot(where, i))
        return (
            pltpu.make_async_copy(bin_.at[i], din.at[:, cols], si.at[i]),
            pltpu.make_async_copy(bdown.at[i], ddown.at[:, cols], sd.at[i]),
        )

    def step(i, carry):
        far_at = far_place(where, i)
        left_at = jnp.where(where[4] == 1, far_at, i)
        for e in range(2):
            sum_in[256 * e : 256 * e + 256, :] = dot(turn[e, :256, :], xo[i, 0])
            sum_down[128 * e : 128 * e + 128, :] = dot(turn[e, 256:, :], xo[i, 1])
        sum_in[left_in, :] += dot(left_turn[0, :256, :], xl[left_at, 0])
        sum_down[left_down, :] += dot(left_turn[0, 256:, :], xl[left_at, 1])
        sum_in[far_in, :] += dot(turn[2, :256, :], xf[far_at, 0])
        sum_down[far_down, :] += dot(turn[2, 256:, :], xf[far_at, 1])
        bin_[i] = narrow(sum_in[...])
        bdown[i] = narrow(sum_down[...])
        for copy in stores(i):
            copy.start()
        return carry

    def finish(i, carry):
        for copy in stores(i):
            copy.wait()
        return carry

    lax.fori_loop(0, 8, step, 0)
    lax.fori_loop(0, 8, finish, 0)


SMEM = pl.BlockSpec(memory_space=pltpu.SMEM)
VMEM = pl.BlockSpec(memory_space=pltpu.VMEM)
FAR_MEMORY = pl.BlockSpec(memory_space=pltpu.HBM)
DMA = pltpu.SemaphoreType.DMA


def shape(*dims, dtype=BF):
    return jax.ShapeDtypeStruct(dims, dtype)


def in_hbm(a):
    return pltpu.with_memory_space_constraint(a, pltpu.HBM)


def params(mib):
    return pltpu.CompilerParams(vmem_limit_bytes=mib * MIB)


QUAD = shape(4, 2, 128, SLICE)
CHUNKS = pltpu.VMEM((8, 2, 128, SLICE), BF)


def shards(tokens, cotangent, routes, gates, fetch, w_in, w_down):
    my_row = lax.axis_index(DP)
    z = lax.axis_index("zhi") * 2 + lax.axis_index("zlo")
    core = lax.axis_index("core")
    plane = my_row % 16
    first, last = plane == 0, plane == 15
    both = jnp.stack([tokens, cotangent])

    candidates = jnp.concatenate(
        [my_row * 2 + jnp.arange(2, dtype=jnp.int32), fetch[my_row]]
    )
    matches = routes[:, :, None] == candidates[None, None, :]
    combine = jnp.sum(jnp.where(matches, gates[:, :, None], 0.0), axis=1)
    need_left = fetch[(my_row + 1) % 32, 0] - my_row * 2
    need_far = fetch[(my_row + 16) % 32, 1] - my_row * 2
    where = jnp.stack([need_left, need_far, z, core, last.astype(jnp.int32)]).astype(jnp.int32)

    def leftward(pairs):
        chosen = [jnp.where(first, got[k - 1], got[k]) for k in pairs]
        return along_plane(jnp.stack(chosen), -1)

    got = {0: both}
    got[-1], got[1] = along_z(both, 1), along_z(both, -1)
    from_far = along_dp(combine[:, 2:4], 16)
    got[-1], got[1], from_far, where = together(got[-1], got[1], from_far, where)
    got[-2], got[2] = along_z(got[-1], 1), along_z(got[1], -1)
    from_left = along_plane(jnp.where(first, from_far[:, 0:1], combine[:, 2:3]), -1)
    got[-2], got[2], from_left = together(got[-2], got[2], from_left)
    weights = jnp.concatenate([combine[:, :2], from_left, from_far[:, 1:2]], axis=1)
    got[-3], got[3] = along_z(got[-2], 1), along_z(got[2], -1)
    early = leftward((0, 2))
    got[-3], got[3], weights = together(got[-3], got[3], weights)
    up, down = along_z(got[-3][0], 1), along_z(got[3][1], -1)
    up, down, early = together(up, down, early)
    got[4] = jnp.stack([up, down])
    own = [got[k] for k in (-2, 0, 2, 4)]
    far = [got[k] for k in (-3, -1, 1, 3)]
    own_peers = [other_core(a) for a in own]
    far_peers = [other_core(a) for a in far]
    got[4], *own_peers = together(got[4], *own_peers)
    own = own[:3] + [got[4]] + [in_hbm(a) for a in own_peers]
    far = far + [in_hbm(a) for a in far_peers]
    late = leftward((-2, 4))

    flat_in = in_hbm(w_in.reshape(512, 4096))
    flat_down = in_hbm(w_down.reshape(256, 4096))
    own_out, own_peer, far_out, far_peer, turn = pl.pallas_call(
        near_kernel,
        out_shape=(QUAD,) * 4 + (shape(3, 384, 128),),
        in_specs=[SMEM, VMEM] + [FAR_MEMORY] * 18,
        out_specs=(VMEM,) * 5,
        scratch_shapes=[
            CHUNKS,
            CHUNKS,
            pltpu.VMEM((8, 512, SLICE), BF),
            pltpu.VMEM((8, 256, SLICE), BF),
            DMA((8,)),
            DMA((8,)),
            DMA((8,)),
            DMA((8,)),
        ],
        compiler_params=params(16),
        name="near",
    )(where, weights, flat_in, flat_down, *own, *far)
    late, turn = together(late, turn)
    lefts = [early, late, other_core(early), other_core(late)]
    left_out, left_peer, left_turn = pl.pallas_call(
        left_kernel,
        out_shape=(QUAD,) * 2 + (shape(1, 384, 128),),
        in_specs=[SMEM, VMEM] + [FAR_MEMORY] * 6,
        out_specs=(VMEM,) * 3,
        scratch_shapes=[
            CHUNKS,
            pltpu.VMEM((8, 256, SLICE), BF),
            pltpu.VMEM((8, 128, SLICE), BF),
            DMA((8,)),
            DMA((8,)),
            DMA((8,)),
        ],
        compiler_params=params(10),
        name="left",
    )(where, weights, flat_in, flat_down, *lefts)
    own_peer, far_peer = other_core(own_peer), other_core(far_peer)
    left_peer = other_core(left_peer)

    def left_sum(i):
        return wide(left_out[i]) + wide(left_peer[i])

    def rightward(sums):
        return along_plane(narrow(sums), 1)

    right = {0: rightward(left_sum(0))}
    moved = lax.ppermute(narrow(left_sum(3)), "zhi", [(i, (i + 2) % 4) for i in range(4)])
    grad_in, grad_down = pl.pallas_call(
        weights_kernel,
        out_shape=(shape(512, 4096), shape(256, 4096)),
        in_specs=[SMEM, VMEM, VMEM] + [FAR_MEMORY] * 20,
        out_specs=(FAR_MEMORY, FAR_MEMORY),
        scratch_shapes=[
            CHUNKS,
            CHUNKS,
            CHUNKS,
            pltpu.VMEM((512, SLICE), jnp.float32),
            pltpu.VMEM((256, SLICE), jnp.float32),
            pltpu.VMEM((8, 512, SLICE), BF),
            pltpu.VMEM((8, 256, SLICE), BF),
            DMA((8,)),
            DMA((8,)),
            DMA((8,)),
            DMA((8,)),
            DMA((8,)),
        ],
        compiler_params=params(16),
        name="weights",
    )(where, turn, left_turn, *own, *lefts, *far)

    def near_part(i):
        part = wide(own_out[i]) + wide(own_peer[i])
        return part + jnp.where(first, 0.0, wide(right[i])) if i in right else part

    def far_part(i):
        part = wide(far_out[i]) + wide(far_peer[i])
        return part + jnp.where(first, wide(right[i]), 0.0) if i in right else part

    top = narrow(near_part(3))
    up, down = along_z(top[0], 1), along_z(top[1], -1)
    up, down, right[0], moved, grad_in, grad_down = together(
        up, down, right[0], moved, grad_in, grad_down
    )
    high, low = far_part(3), far_part(0)
    up = narrow(jnp.stack([high[0] + wide(up), high[1]]))
    down = narrow(jnp.stack([low[0], low[1] + wide(down)]))
    up, down = along_z(up, 1), along_z(down, -1)
    right[2] = rightward(left_sum(2))
    up, down, right[2] = together(up, down, right[2])
    up, down = narrow(near_part(2) + wide(up)), narrow(near_part(0) + wide(down))
    up, down = along_z(up, 1), along_z(down, -1)
    right[1] = rightward(left_sum(1) + wide(moved))
    up, down, right[1] = together(up, down, right[1])
    up, down = narrow(far_part(2) + wide(up)), narrow(far_part(1) + wide(down))
    up, down = along_z(up, 1), along_z(down, -1)
    total = narrow(near_part(1) + wide(up) + wide(down))
    return total[0], total[1], grad_in.reshape(w_in.shape), grad_down.reshape(w_down.shape)


def solution(mesh):
    fine = Mesh(mesh.devices.reshape(2, 4, 4, 4, 2), AXES)
    return jax.shard_map(
        shards,
        mesh=fine,
        in_specs=(
            P(DP, HID),
            P(DP, HID),
            P(DP, None),
            P(DP, None),
            P(),
            P(DP, None, HID, None),
            P(DP, HID, None),
        ),
        out_specs=(
            P(DP, HID),
            P(DP, HID),
            P(DP, None, HID, None),
            P(DP, HID, None),
        ),
        check_vma=False,
    )
```
